128 devices in a mesh: aa: 4 (over z_lo, core), ba: 32 (over y, z_hi, x).
Axes of the slice: x: 4, y: 4, z: 4 (z_hi: 2, z_lo: 2; z = z_hi * 2 + z_lo), core: 2. Of those that a mesh axis runs over, the one named last changes fastest.
Arguments:
- hidden: bfloat16 [512, 3072], P('aa'), may hold values from -24 to 24
- head_weight: bfloat16 [3072, 32, 4, 512], P(None, 'ba'), as said below
- teacher: bfloat16 [512, 4, 32, 512], P('ba', 'aa'), may hold values from -60 to 250
Outputs:
- divergence: float32 [], replicated
- grad_hidden: bfloat16 [512, 3072], P('aa')
- grad_head: bfloat16 [3072, 32, 4, 512], P('aa', 'ba')
The draws below stay inside these ranges and needn't reach their ends.
Inputs may be any that keep to these rules, and one draw needn't show every extreme that they name: `head_weight`: entries of order one over the square root of 3072.
All inputs are finite; a program needn't handle non-finite values.
Results may differ from the reference program's by a relative error of at most 0.0049.
Values may be sent and summed in bfloat16 or wider, within the bound.
A program may use at most 128 MiB of HBM per device.

```python
import math
import jax
import jax.numpy as jnp
from jax import lax

D = 3072
V = 65536
TOKENS = 512
VPIECE = 512
N_AA = 4
N_BA = 32


def draw_hidden(key, part):
    values = jnp.clip(jax.random.normal(jax.random.fold_in(key, 31), (TOKENS, D), jnp.float32), -6.0, 6.0)
    return jnp.clip(values, -24.0, 24.0).astype(jnp.bfloat16)


def draw_head_weight(key, part):
    noise = jnp.clip(jax.random.normal(jax.random.fold_in(key, 41), (D, N_BA, N_AA, VPIECE), jnp.float32), -6.0, 6.0)
    spread = jnp.sqrt(1.0 + 2.2 * jnp.arange(N_BA, dtype=jnp.float32) / max(N_BA - 1, 1))
    weight = noise * spread[None, :, None, None] / math.sqrt(D)
    return weight.astype(jnp.bfloat16)


def draw_teacher(key, part):
    noise = jnp.clip(jax.random.normal(jax.random.fold_in(key, 51), (TOKENS, N_AA, N_BA, VPIECE), jnp.float32), -6.0, 6.0)
    rising = math.log(3.0) * jnp.arange(N_BA, dtype=jnp.float32) / max(N_BA - 1, 1)
    logits = 3.0 * noise + rising[None, None, :, None]
    return jnp.clip(logits, -60.0, 250.0).astype(jnp.bfloat16)


def setup_inputs(seed: int = 0) -> dict:
    key_of = jax.random.split(jax.random.key(seed), 4)
    hidden = draw_hidden(jax.random.fold_in(key_of[3], 71), 0)
    head_weight = draw_head_weight(jax.random.fold_in(key_of[3], 71), 0)
    teacher = draw_teacher(jax.random.fold_in(key_of[3], 71), 0)
    return {"hidden": hidden, "head_weight": head_weight, "teacher": teacher}


grad_scale = 256.0


def reference(hidden, head_weight, teacher):
    ordered = jnp.transpose(head_weight, (0, 2, 1, 3)).reshape(D, V)
    student = jnp.dot(hidden, ordered, preferred_element_type=jnp.float32)
    student_peak = jnp.max(student, axis=1, keepdims=True)
    student_total = jnp.sum(jnp.exp(student - student_peak), axis=1, keepdims=True)
    log_student = (student - student_peak) - jnp.log(student_total)
    target = teacher.reshape(TOKENS, V).astype(jnp.float32)
    target_peak = jnp.max(target, axis=1, keepdims=True)
    target_total = jnp.sum(jnp.exp(target - target_peak), axis=1, keepdims=True)
    log_target = (target - target_peak) - jnp.log(target_total)
    student_prob = jnp.exp(log_student)
    target_prob = jnp.exp(log_target)
    divergence = jnp.sum(target_prob * (log_target - log_student)) / TOKENS
    gradient = (grad_scale * (student_prob - target_prob)).astype(jnp.bfloat16)
    grad_hidden = lax.dot_general(gradient, ordered, (((1,), (1,)), ((), ())), preferred_element_type=jnp.float32).astype(jnp.bfloat16)
    grad_ordered = lax.dot_general(hidden, gradient, (((0,), (0,)), ((), ())), preferred_element_type=jnp.float32)
    grad_head = jnp.transpose(grad_ordered.reshape(D, N_AA, N_BA, VPIECE), (0, 2, 1, 3)).astype(jnp.bfloat16)
    return divergence, grad_hidden, grad_head
```

```python
import functools

import jax
import jax.numpy as jnp
from jax import lax
from jax.experimental import pallas as pl
from jax.experimental.pallas import tpu as pltpu
from jax.sharding import PartitionSpec as P

MESH = pl.DeviceIdType.MESH
F32 = jnp.float32
BF16 = jnp.bfloat16
grad_scale = 256.0
N_CHUNKS = 12
TB = 16
PAD = 128


def lanes_to_rows(row, n):
    return jnp.transpose(jnp.broadcast_to(row, (n, n)))


def kernel(
    n_ba, x_size,
    hid_hbm, w_hbm, t_hbm,
    div_ref, gh_out, gw_out,
    hid, w_raw, w_std, w_tr, t_raw, t_send, t_in, stu, lse_buf,
    hall, gall, acc, gw, part, rs_buf, z_send, z_recv, fin, kl_p, kl_z, kl_a,
    in_sem, w_sem, t_ssem, t_rsem, h_ssem, h_rsem, s_ssem, s_rsem,
    g_ssem, g_rsem, f_ssem, f_rsem, r_ssem, r_rsem, z_ssem, z_rsem, a_ssem, a_rsem,
    kp_ssem, kp_rsem, kz_ssem, kz_rsem, ka_ssem, ka_rsem, o_sem,
):
    a = lax.axis_index("aa")
    b = lax.axis_index("ba")
    width = hid.shape[1]
    rows = hid.shape[0]
    piece = w_raw.shape[3]
    per_a = n_ba // 4
    plane = n_ba // 2
    share = width // 4
    n_fb = plane // per_a
    fb_width = width // n_fb
    chunk = w_raw.shape[1]
    t_owner = b // per_a
    t_slot = b % per_a
    zh = (b // x_size) % 2
    p = (b // (2 * x_size)) * x_size + b % x_size
    half = a // 2

    def plane_peer(q):
        return ((q // x_size) * 2 + zh) * x_size + q % x_size

    b_across = plane_peer(p) + (1 - 2 * zh) * x_size
    core_mate = a + 1 - 2 * (a % 2)
    chip_mate = (a + 2) % 4

    def remote(src, dst, ssem, rsem, to_a, to_b):
        return pltpu.make_async_remote_copy(
            src_ref=src, dst_ref=dst, send_sem=ssem, recv_sem=rsem,
            device_id=(to_a, to_b), device_id_type=MESH,
        )

    t_load = pltpu.make_async_copy(t_hbm.at[:, 0], t_raw, in_sem.at[0])
    h_load = pltpu.make_async_copy(hid_hbm, hid, in_sem.at[1])
    t_load.start()
    h_load.start()

    def w_load(k):
        return pltpu.make_async_copy(
            w_hbm.at[pl.ds(k * chunk, chunk), 0], w_raw.at[k], w_sem.at[k]
        )

    for k in range(N_CHUNKS):
        w_load(k).start()

    barrier = pltpu.get_barrier_semaphore()

    def greet(to_a, to_b):
        pl.semaphore_signal(barrier, inc=1, device_id=(to_a, to_b), device_id_type=MESH)

    def greet_peers(k, c):
        src_a, src_b = k // per_a, a * per_a + k % per_a

        @pl.when(jnp.logical_or(src_a != a, src_b != b))
        def _():
            greet(src_a, src_b)

        @pl.when(k != b)
        def _():
            greet(a, k)

        return c

    lax.fori_loop(0, n_ba, greet_peers, 0)
    for step in range(1, 4):
        greet((a + step) % 4, b)

    t_load.wait()
    t_send[:, :, 0:piece] = pltpu.einshape("tjr->jtr", t_raw[...])

    def t_max(j, m):
        return jnp.maximum(m, t_send[j, :, 0:piece].astype(F32))

    t_peak = lax.fori_loop(1, n_ba, t_max, t_send[0, :, 0:piece].astype(F32))
    t_peak = jnp.max(t_peak, axis=1, keepdims=True)

    def t_sum(j, s):
        return s + jnp.exp(t_send[j, :, 0:piece].astype(F32) - t_peak)

    t_total = lax.fori_loop(0, n_ba, t_sum, jnp.zeros((TB, piece), F32))
    t_lse = t_peak + jnp.log(jnp.sum(t_total, axis=1, keepdims=True))
    hi = t_lse.astype(BF16).astype(F32)
    mid = (t_lse - hi).astype(BF16).astype(F32)
    low = t_lse - hi - mid
    lane = lax.broadcasted_iota(jnp.int32, (TB, PAD), 1)
    tail = jnp.where(lane == 0, hi, jnp.where(lane == 1, mid, low)).astype(BF16)

    def t_tail(j, c):
        t_send[j, :, piece : piece + PAD] = tail
        return c

    lax.fori_loop(0, n_ba, t_tail, 0)

    def relayout(k, c):
        w_load(k).wait()
        at = pl.ds(pl.multiple_of(k * chunk, chunk), chunk)
        w_std[:, at, :] = pltpu.einshape("dir->idr", w_raw[k])
        return c

    early = 8
    lax.fori_loop(0, early, relayout, 0)

    expected = 2 * n_ba - 1 + 3 - jnp.where(t_owner == a, 1, 0)
    pl.semaphore_wait(barrier, expected)

    def t_copy(k):
        return remote(
            t_send.at[k], t_in.at[a, pl.ds(pl.multiple_of(t_slot * TB, TB), TB)],
            t_ssem.at[k], t_rsem.at[a, t_slot], t_owner, k,
        )

    def t_self(k):
        return jnp.logical_and(t_owner == a, k == b)

    def t_start(k, c):
        @pl.when(t_self(k))
        def _():
            pltpu.make_async_copy(
                t_send.at[k],
                t_in.at[a, pl.ds(pl.multiple_of(t_slot * TB, TB), TB)],
                t_rsem.at[a, t_slot],
            ).start()

        @pl.when(jnp.logical_not(t_self(k)))
        def _():
            t_copy(k).start()

        return c

    lax.fori_loop(0, n_ba, t_start, 0)

    lax.fori_loop(early, N_CHUNKS, relayout, 0)
    h_load.wait()
    for i in range(4):
        stu[:, i * piece : (i + 1) * piece] = jnp.dot(
            hid[...], w_std[i], preferred_element_type=F32
        )
    s = stu[...]
    s_peak = jnp.max(s, axis=1, keepdims=True)
    s_total = jnp.sum(jnp.exp(s - s_peak), axis=1, keepdims=True)
    s_part = s_peak + jnp.log(s_total)
    lse_buf[b] = jnp.transpose(jnp.broadcast_to(s_part, (rows, rows)))[0:1, :]

    def h_copy(step):
        to = (a + step) % 4
        return remote(
            hid_hbm.at[:, pl.ds(pl.multiple_of(to * share, share), share)],
            hall.at[pl.ds(pl.multiple_of(a * rows, rows), rows)],
            h_ssem.at[step - 1], h_rsem.at[a], to, b,
        )

    h_own = pltpu.make_async_copy(
        hid_hbm.at[:, pl.ds(pl.multiple_of(a * share, share), share)],
        hall.at[pl.ds(pl.multiple_of(a * rows, rows), rows)],
        h_rsem.at[a],
    )

    def s_copy(k):
        return remote(lse_buf.at[b], lse_buf.at[b], s_ssem.at[k], s_rsem.at[b], a, k)

    def s_start(k, c):
        @pl.when(k != b)
        def _():
            s_copy(k).start()

        return c

    lax.fori_loop(0, n_ba, s_start, 0)
    for step in range(1, 4):
        h_copy(step).start()
    h_own.start()

    def turn(k, c):
        at = pl.ds(pl.multiple_of(k * chunk, chunk), chunk)
        for i in range(4):
            w_tr[i, :, at] = jnp.transpose(w_std[i, at, :])
        return c

    lax.fori_loop(0, N_CHUNKS, turn, 0)

    def s_wait(k, c):
        @pl.when(k != b)
        def _():
            remote(lse_buf.at[k], lse_buf.at[k], s_ssem.at[k], s_rsem.at[k], a, k).wait_recv()

        return c

    lax.fori_loop(0, n_ba, s_wait, 0)
    parts = lse_buf[...]
    s_top = jnp.max(parts, axis=0)
    s_lse = s_top + jnp.log(jnp.sum(jnp.exp(parts - s_top[None]), axis=0))
    s_lse = lanes_to_rows(s_lse, rows)[:, 0:1]

    def t_wait(k, c):
        src = t_in.at[k // per_a, pl.ds(pl.multiple_of((k % per_a) * TB, TB), TB)]
        remote(t_send.at[0], src, t_ssem.at[0], t_rsem.at[k // per_a, k % per_a], a, b).wait_recv()
        return c

    lax.fori_loop(0, n_ba, t_wait, 0)
    t_parts = []
    for i in range(4):
        code = t_in[i, :, piece : piece + PAD].astype(F32)
        t_parts.append(code[:, 0:1] + code[:, 1:2] + code[:, 2:3])
    t_top = jnp.maximum(jnp.maximum(t_parts[0], t_parts[1]), jnp.maximum(t_parts[2], t_parts[3]))
    t_tot = sum(jnp.exp(v - t_top) for v in t_parts)
    t_all = t_top + jnp.log(t_tot)

    mine = pl.ds(pl.multiple_of(a * rows, rows), rows)

    def g_copy(i, src_a, to_a, ssem, rsem):
        at = pl.ds(pl.multiple_of(src_a * rows, rows), rows)
        return remote(gall.at[i, at], gall.at[i, at], ssem, rsem, to_a, b)

    def g_core(i):
        return g_copy(i, a, core_mate, g_ssem.at[0, i], g_rsem.at[0, i])

    def g_chip(i):
        return g_copy(i, a, chip_mate, g_ssem.at[1, i], g_rsem.at[1, i])

    def g_pass(i):
        return g_copy(i, chip_mate, core_mate, f_ssem.at[i], f_rsem.at[i])

    kl = jnp.zeros((rows, 128), F32)
    for i in range(4):
        log_target = t_in[i, :, 0:piece].astype(F32) - t_all
        log_student = stu[:, i * piece : (i + 1) * piece] - s_lse
        target_prob = jnp.exp(log_target)
        student_prob = jnp.exp(log_student)
        gall[i, mine, :] = (grad_scale * (student_prob - target_prob)).astype(BF16)
        term = target_prob * (log_target - log_student)
        for v in range(piece // 128):
            kl = kl + term[:, v * 128 : (v + 1) * 128]
        if i > 0:
            g_chip(i - 1).start()
            g_core(i - 1).start()
    kl_p[p] = jnp.sum(kl, axis=0, keepdims=True)
    g_chip(3).start()
    g_core(3).start()

    def r_block(q):
        return part.at[
            pl.ds(pl.multiple_of((q % per_a) * TB, TB), TB),
            pl.ds(pl.multiple_of((q // per_a) * fb_width, fb_width), fb_width),
        ]

    def r_copy(q):
        return remote(r_block(q), rs_buf.at[p], r_ssem.at[q], r_rsem.at[p], a, plane_peer(q))

    def kp_copy(q):
        return remote(kl_p.at[p], kl_p.at[p], kp_ssem.at[q], kp_rsem.at[p], a, plane_peer(q))

    r_own = pltpu.make_async_copy(r_block(p), rs_buf.at[p], r_rsem.at[p])

    def r_start(q, c):
        @pl.when(q == p)
        def _():
            r_own.start()

        @pl.when(q != p)
        def _():
            r_copy(q).start()

        return c

    def kp_start(q, c):
        @pl.when(q != p)
        def _():
            kp_copy(q).start()

        return c

    for f in range(n_fb):
        cols = slice(f * fb_width, (f + 1) * fb_width)
        total = None
        for i in range(4):
            term = jnp.dot(gall[i, mine, :], w_tr[i, :, cols], preferred_element_type=F32)
            total = term if total is None else total + term
        part[:, cols] = total.astype(BF16)
        lax.fori_loop(f * per_a, (f + 1) * per_a, r_start, 0)
    lax.fori_loop(0, plane, kp_start, 0)

    h_own.wait()
    for step in range(1, 4):
        src = (a + step) % 4
        remote(
            hid_hbm.at[:, pl.ds(0, share)],
            hall.at[pl.ds(pl.multiple_of(src * rows, rows), rows)],
            h_ssem.at[0], h_rsem.at[src], src, b,
        ).wait_recv()
    near = pl.ds(pl.multiple_of(half * 2 * rows, 2 * rows), 2 * rows)
    far = pl.ds(pl.multiple_of((1 - half) * 2 * rows, 2 * rows), 2 * rows)

    def outer(i, at):
        return lax.dot_general(
            hall[at, :], gall[i, at, :], (((0,), (0,)), ((), ())), preferred_element_type=F32
        )

    def got_core(i):
        g_copy(i, core_mate, core_mate, g_ssem.at[0, i], g_rsem.at[0, i]).wait_recv()

    def got_chip(i):
        g_copy(i, chip_mate, chip_mate, g_ssem.at[1, i], g_rsem.at[1, i]).wait_recv()
        g_pass(i).start()

    def got_pass(i):
        g_copy(i, 3 - a, core_mate, f_ssem.at[i], f_rsem.at[i]).wait_recv()

    for i in range(4):
        got_core(i)
        acc[i] = outer(i, near)
    got_chip(0)
    got_chip(1)
    got_chip(2)

    def r_wait(q, c):
        @pl.when(q == p)
        def _():
            r_own.wait()

        @pl.when(q != p)
        def _():
            remote(r_block(q), rs_buf.at[q], r_ssem.at[q], r_rsem.at[q], a, b).wait_recv()
            remote(kl_p.at[q], kl_p.at[q], kp_ssem.at[q], kp_rsem.at[q], a, b).wait_recv()

        return c

    lax.fori_loop(0, plane, r_wait, 0)

    def r_sum(q, total):
        return total + rs_buf[q].astype(F32)

    z_send[...] = lax.fori_loop(0, plane, r_sum, jnp.zeros((TB, fb_width), F32)).astype(BF16)
    kl_z[zh] = jnp.sum(kl_p[...], axis=0)
    z_copy = remote(z_send, z_recv, z_ssem, z_rsem, a, b_across)
    kz_copy = remote(kl_z.at[zh], kl_z.at[zh], kz_ssem, kz_rsem, a, b_across)
    z_copy.start()
    kz_copy.start()
    got_chip(3)
    z_copy.wait_recv()
    fin[...] = (z_send[...].astype(F32) + z_recv[...].astype(F32)).astype(BF16)
    remote(kl_z.at[1 - zh], kl_z.at[1 - zh], kz_ssem, kz_rsem, a, b_across).wait_recv()
    kl_a[a] = jnp.sum(kl_z[...], axis=0)

    def out_block(q):
        return gh_out.at[
            pl.ds(pl.multiple_of((q % per_a) * TB, TB), TB),
            pl.ds(pl.multiple_of((q // per_a) * fb_width, fb_width), fb_width),
        ]

    def a_copy(q):
        return remote(fin, out_block(p), a_ssem.at[q], a_rsem.at[p], a, plane_peer(q))

    a_own = pltpu.make_async_copy(fin, out_block(p), a_rsem.at[p])

    def a_start(q, c):
        @pl.when(q == p)
        def _():
            a_own.start()

        @pl.when(q != p)
        def _():
            a_copy(q).start()

        return c

    lax.fori_loop(0, plane, a_start, 0)

    def ka_copy(step):
        return remote(
            kl_a.at[a], kl_a.at[a], ka_ssem.at[step - 1], ka_rsem.at[a], (a + step) % 4, b
        )

    for step in range(1, 4):
        ka_copy(step).start()

    for i in range(4):
        got_pass(i)
        gw[i] = (acc[i] + outer(i, far)).astype(BF16)
    n_out = share // chunk
    gw_store = [
        pltpu.make_async_copy(w_raw.at[k], gw_out.at[pl.ds(k * chunk, chunk)], o_sem.at[k])
        for k in range(n_out)
    ]
    for k in range(n_out):
        w_raw[k] = pltpu.einshape("idr->dir", gw[:, k * chunk : (k + 1) * chunk, :])
        gw_store[k].start()

    for step in range(1, 4):
        src = (a + step) % 4
        remote(kl_a.at[src], kl_a.at[src], ka_ssem.at[0], ka_rsem.at[src], src, b).wait_recv()
    summed = jnp.sum(kl_a[...], axis=0)
    div_ref[...] = jnp.broadcast_to(
        jnp.sum(summed, axis=1, keepdims=True) / (4.0 * rows), div_ref.shape
    )

    def a_wait(q, c):
        @pl.when(q == p)
        def _():
            a_own.wait()

        @pl.when(q != p)
        def _():
            remote(fin, out_block(q), a_ssem.at[q], a_rsem.at[q], a, b).wait_recv()

        return c

    lax.fori_loop(0, plane, a_wait, 0)
    for k in range(n_out):
        gw_store[k].wait()

    def sent_ba(k, c):
        @pl.when(jnp.logical_not(t_self(k)))
        def _():
            t_copy(k).wait_send()

        @pl.when(k != b)
        def _():
            s_copy(k).wait_send()

        return c

    lax.fori_loop(0, n_ba, sent_ba, 0)

    def sent_plane(q, c):
        @pl.when(q != p)
        def _():
            r_copy(q).wait_send()
            kp_copy(q).wait_send()
            a_copy(q).wait_send()

        return c

    lax.fori_loop(0, plane, sent_plane, 0)
    for step in range(1, 4):
        h_copy(step).wait_send()
        ka_copy(step).wait_send()
    for i in range(4):
        g_core(i).wait_send()
        g_chip(i).wait_send()
        g_pass(i).wait_send()
    z_copy.wait_send()
    kz_copy.wait_send()


def on_device(n_ba, hidden, head_weight, teacher):
    rows, width = hidden.shape
    piece = head_weight.shape[3]
    share = width // 4
    plane = n_ba // 2
    per_a = n_ba // 4
    fb_width = width // (plane // per_a)
    chunk = width // N_CHUNKS
    x_size = 4 if n_ba == 32 else 1
    dma = pltpu.SemaphoreType.DMA
    out = pl.pallas_call(
        functools.partial(kernel, n_ba, x_size),
        out_shape=(
            jax.ShapeDtypeStruct((8, 128), F32),
            jax.ShapeDtypeStruct((rows, width), BF16),
            jax.ShapeDtypeStruct((share, 4, piece), BF16),
        ),
        in_specs=[pl.BlockSpec(memory_space=pl.ANY)] * 3,
        out_specs=(
            pl.BlockSpec(memory_space=pltpu.VMEM),
            pl.BlockSpec(memory_space=pl.ANY),
            pl.BlockSpec(memory_space=pl.ANY),
        ),
        scratch_shapes=[
            pltpu.VMEM((rows, width), BF16),
            pltpu.VMEM((N_CHUNKS, chunk, 4, piece), BF16),
            pltpu.VMEM((4, width, piece), BF16),
            pltpu.VMEM((4, piece, width), BF16),
            pltpu.VMEM((TB, n_ba, piece), BF16),
            pltpu.VMEM((n_ba, TB, piece + PAD), BF16),
            pltpu.VMEM((4, rows, piece + PAD), BF16),
            pltpu.VMEM((rows, 4 * piece), F32),
            pltpu.VMEM((n_ba, 1, rows), F32),
            pltpu.VMEM((4 * rows, share), BF16),
            pltpu.VMEM((4, 4 * rows, piece), BF16),
            pltpu.VMEM((4, share, piece), F32),
            pltpu.VMEM((4, share, piece), BF16),
            pltpu.VMEM((rows, width), BF16),
            pltpu.VMEM((plane, TB, fb_width), BF16),
            pltpu.VMEM((TB, fb_width), BF16),
            pltpu.VMEM((TB, fb_width), BF16),
            pltpu.VMEM((TB, fb_width), BF16),
            pltpu.VMEM((plane, 1, 128), F32),
            pltpu.VMEM((2, 1, 128), F32),
            pltpu.VMEM((4, 1, 128), F32),
            dma((2,)), dma((N_CHUNKS,)),
            dma((n_ba,)), dma((4, per_a)),
            dma((3,)), dma((4,)),
            dma((n_ba,)), dma((n_ba,)),
            dma((2, 4)), dma((2, 4)),
            dma((4,)), dma((4,)),
            dma((plane,)), dma((plane,)),
            dma, dma,
            dma((plane,)), dma((plane,)),
            dma((plane,)), dma((plane,)),
            dma, dma,
            dma((3,)), dma((4,)),
            dma((share // chunk,)),
        ],
        compiler_params=pltpu.CompilerParams(
            collective_id=0, has_side_effects=True, vmem_limit_bytes=66_000_000
        ),
    )(hidden, head_weight, teacher)
    return out[0][0, 0], out[1], out[2][:, None]


def solution(mesh):
    placed = (P("aa", None), P(None, "ba", None, None), P("ba", "aa", None, None))
    return jax.shard_map(
        functools.partial(on_device, mesh.shape["ba"]),
        mesh=mesh,
        in_specs=placed,
        out_specs=(P(), P("aa", None), P("aa", "ba", None, None)),
        check_vma=False,
    )
```

```python
import functools

import jax
import jax.numpy as jnp
from jax import lax
from jax.experimental import pallas as pl
from jax.experimental.pallas import tpu as pltpu
from jax.sharding import PartitionSpec as P

MESH = pl.DeviceIdType.MESH
F32 = jnp.float32
BF16 = jnp.bfloat16
grad_scale = 256.0
N_CHUNKS = 6
STORES = 6
VMEM_LIMIT = 58_000_000
TB = 16
HALVES = 2


def finish(pending):
    for wait in pending:
        wait()


def lanes_to_rows(row, n):
    return jnp.transpose(jnp.broadcast_to(row, (n, n)))


def kernel(
    n_ba, x_size,
    hid_hbm, w_hbm, t_hbm,
    div_ref, gh_out, gw_out,
    hid, w_raw, w_std, w_tr, t_raw, t_send, t_in, stu, lse_buf, n_send, n_in,
    hall, gall, acc, part, rs_buf, z_send, z_recv, fin, kl_p, kl_z, kl_a,
    in_sem, w_sem, t_ssem, t_rsem, n_ssem, n_rsem, h_ssem, h_rsem, s_ssem, s_rsem,
    g_ssem, g_rsem, r_ssem, r_rsem, z_ssem, z_rsem, a_ssem, a_rsem,
    kp_ssem, kp_rsem, kz_ssem, kz_rsem, ka_ssem, ka_rsem,
):
    a = lax.axis_index("aa")
    b = lax.axis_index("ba")
    width = hid.shape[1]
    rows = hid.shape[0]
    piece = w_raw.shape[3]
    per_a = n_ba // 4
    plane = n_ba // 2
    share = width // 4
    n_fb = plane // per_a
    fb_width = width // n_fb // HALVES
    chunk = w_raw.shape[1]
    t_owner = b // per_a
    t_slot = b % per_a
    zh = (b // x_size) % 2
    p = (b // (2 * x_size)) * x_size + b % x_size
    half = a // 2

    def plane_peer(q):
        return ((q // x_size) * 2 + zh) * x_size + q % x_size

    b_across = plane_peer(p) + (1 - 2 * zh) * x_size
    core_mate = a + 1 - 2 * (a % 2)
    chip_mate = (a + 2) % 4

    def remote(src, dst, ssem, rsem, to_a, to_b):
        return pltpu.make_async_remote_copy(
            src_ref=src, dst_ref=dst, send_sem=ssem, recv_sem=rsem,
            device_id=(to_a, to_b), device_id_type=MESH,
        )

    pending = []

    def drain(sem, like):
        pending.append(remote(like, like, sem, sem, a, b).wait_send)

    def drain_t(sem, ref):
        def wait():
            @pl.when(t_owner == a)
            def _():
                remote(ref.at[: n_ba - 1], ref.at[: n_ba - 1], sem, sem, a, b).wait_send()

            @pl.when(t_owner != a)
            def _():
                remote(ref, ref, sem, sem, a, b).wait_send()

        pending.append(wait)

    t_load = pltpu.make_async_copy(t_hbm.at[:, 0], t_raw, in_sem.at[0])
    h_load = pltpu.make_async_copy(hid_hbm, hid, in_sem.at[1])
    t_load.start()

    def w_load(k):
        return pltpu.make_async_copy(
            w_hbm.at[pl.ds(k * chunk, chunk), 0], w_raw.at[k], w_sem.at[k]
        )

    h_load.start()
    for k in range(N_CHUNKS):
        w_load(k).start()

    barrier = pltpu.get_barrier_semaphore()

    def greet(to_a, to_b):
        pl.semaphore_signal(barrier, inc=1, device_id=(to_a, to_b), device_id_type=MESH)

    for step in range(n_ba):
        src_a, src_b = (a + step // per_a) % 4, a * per_a + (b + step) % per_a
        if step:
            greet(src_a, src_b)
        else:

            @pl.when(t_owner != a)
            def _():
                greet(src_a, src_b)

    for step in range(1, n_ba):
        greet(a, (b + step) % n_ba)
    for step in range(1, 4):
        greet((a + step) % 4, b)

    t_load.wait()
    t_send[...] = pltpu.einshape("tjr->jtr", t_raw[...])
    expected = 2 * n_ba - 1 + 3 - jnp.where(t_owner == a, 1, 0)
    pl.semaphore_wait(barrier, expected)
    t_dst = t_in.at[a, pl.ds(pl.multiple_of(t_slot * TB, TB), TB)]

    def to_owner(src_of, dst, ssem, rsem):
        for step in range(n_ba):
            k = (b + step) % n_ba
            copy = remote(src_of(k), dst, ssem, rsem, t_owner, k)
            if step:
                copy.start()
            else:

                @pl.when(t_owner != a)
                def _():
                    copy.start()

                @pl.when(t_owner == a)
                def _():
                    pltpu.make_async_copy(src_of(k), dst, rsem).start()

    to_owner(lambda k: t_send.at[k], t_dst, t_ssem, t_rsem)
    drain_t(t_ssem, t_send)

    def t_max(j, m):
        return jnp.maximum(m, t_send[j].astype(F32))

    t_peak = lax.fori_loop(1, n_ba, t_max, t_send[0].astype(F32))
    t_peak = jnp.max(t_peak, axis=1, keepdims=True)

    def t_sum(j, s):
        return s + jnp.exp(t_send[j].astype(F32) - t_peak)

    t_total = lax.fori_loop(0, n_ba, t_sum, jnp.zeros((TB, piece), F32))
    t_lse = t_peak + jnp.log(jnp.sum(t_total, axis=1, keepdims=True))
    token = lax.broadcasted_iota(jnp.int32, (TB, rows), 0)
    lane = lax.broadcasted_iota(jnp.int32, (TB, rows), 1)
    n_send[...] = jnp.sum(
        jnp.where(lane == token + t_slot * TB, t_lse, 0.0), axis=0, keepdims=True
    )

    to_owner(lambda k: n_send, n_in.at[a, t_slot], n_ssem, n_rsem)
    drain_t(n_ssem, lse_buf)

    sub = chunk // 2

    def relayout(k, c):
        at = pl.ds(pl.multiple_of(k * sub, sub), sub)
        w_std[:, at, :] = pltpu.einshape(
            "dir->idr", w_raw[k // 2, pl.ds(pl.multiple_of((k % 2) * sub, sub), sub)]
        )
        return c

    h_load.wait()
    for part_of in range(2):
        for k in range(part_of * N_CHUNKS // 2, (part_of + 1) * N_CHUNKS // 2):
            w_load(k).wait()
            lax.fori_loop(2 * k, 2 * k + 2, relayout, 0)
        deep = slice(part_of * width // 2, (part_of + 1) * width // 2)
        for i in range(4):
            at = slice(i * piece, (i + 1) * piece)
            product = jnp.dot(hid[:, deep], w_std[i, deep], preferred_element_type=F32)
            stu[:, at] = product if part_of == 0 else stu[:, at] + product
    s = stu[...]
    s_peak = jnp.max(s, axis=1, keepdims=True)
    s_total = jnp.sum(jnp.exp(s - s_peak), axis=1, keepdims=True)
    s_part = s_peak + jnp.log(s_total)
    lse_buf[b] = jnp.transpose(jnp.broadcast_to(s_part, (rows, rows)))[0:1, :]

    for step in range(1, n_ba):
        remote(lse_buf.at[b], lse_buf.at[b], s_ssem, s_rsem, a, (b + step) % n_ba).start()
    drain(s_ssem, lse_buf.at[: n_ba - 1])

    mine = pl.ds(pl.multiple_of(a * rows, rows), rows)

    def h_cols(to):
        return hid_hbm.at[:, pl.ds(pl.multiple_of(to * share, share), share)]

    for step in range(1, 4):
        to = (a + step) % 4
        remote(h_cols(to), hall.at[mine], h_ssem, h_rsem, to, b).start()
    pltpu.make_async_copy(h_cols(a), hall.at[mine], h_rsem).start()
    drain(h_ssem, hall.at[: 3 * rows])

    def turn(k, c):
        at = pl.ds(pl.multiple_of(k * sub, sub), sub)
        for i in range(4):
            w_tr[i, :, at] = jnp.transpose(w_std[i, at, :])
        return c

    lax.fori_loop(0, 2 * N_CHUNKS, turn, 0)

    def arrived(sem, like):
        remote(like, like, sem, sem, a, b).wait_recv()

    arrived(s_rsem, lse_buf.at[: n_ba - 1])
    parts = lse_buf[...]
    s_top = jnp.max(parts, axis=0)
    s_lse = s_top + jnp.log(jnp.sum(jnp.exp(parts - s_top[None]), axis=0))
    s_lse = lanes_to_rows(s_lse, rows)[:, 0:1]

    arrived(t_rsem, t_in)
    arrived(n_rsem, n_in)
    t_parts = jnp.sum(n_in[...], axis=1)
    t_top = jnp.max(t_parts, axis=0)
    t_all = t_top + jnp.log(jnp.sum(jnp.exp(t_parts - t_top[None]), axis=0))
    t_all = lanes_to_rows(t_all, rows)[:, 0:1]

    def g_copy(i, src_a, to_a, ssem, rsem):
        at = pl.ds(pl.multiple_of(src_a * rows, rows), rows)
        return remote(gall.at[i, at], gall.at[i, at], ssem, rsem, to_a, b)

    def g_core(i):
        return g_copy(i, a, core_mate, g_ssem.at[0], g_rsem.at[0, i])

    def g_chip(i):
        return g_copy(i, a, chip_mate, g_ssem.at[1], g_rsem.at[1, i])

    def g_pass(i):
        return g_copy(i, chip_mate, core_mate, g_ssem.at[2], g_rsem.at[2, i])

    for k in range(3):
        drain(g_ssem.at[k], gall.at[:, mine])

    kl = jnp.zeros((rows, 128), F32)
    for i in range(4):
        log_target = t_in[i].astype(F32) - t_all
        log_student = stu[:, i * piece : (i + 1) * piece] - s_lse
        target_prob = jnp.exp(log_target)
        student_prob = jnp.exp(log_student)
        gall[i, mine, :] = (grad_scale * (student_prob - target_prob)).astype(BF16)
        term = target_prob * (log_target - log_student)
        for v in range(piece // 128):
            kl = kl + term[:, v * 128 : (v + 1) * 128]
        if i > 0:
            g_chip(i - 1).start()
            g_core(i - 1).start()
    kl_p[p] = jnp.sum(kl, axis=0, keepdims=True)
    g_core(3).start()

    def block_of(ref, q, f):
        return ref.at[
            pl.ds(pl.multiple_of((q % per_a) * TB, TB), TB),
            pl.ds(pl.multiple_of((f * n_fb + q // per_a) * fb_width, fb_width), fb_width),
        ]

    def to_plane(src_of, dst, ssem, rsem):
        for step in range(1, plane):
            q = (p + step) % plane
            remote(src_of(q), dst, ssem, rsem, a, plane_peer(q)).start()

    for f in range(HALVES):
        cols = slice(f * n_fb * fb_width, (f + 1) * n_fb * fb_width)
        total = None
        for i in range(4):
            term = jnp.dot(gall[i, mine, :], w_tr[i, :, cols], preferred_element_type=F32)
            total = term if total is None else total + term
        part[:, cols] = total.astype(BF16)
        to_plane(lambda q: block_of(part, q, f), rs_buf.at[f, p], r_ssem.at[f], r_rsem.at[f])
        pltpu.make_async_copy(block_of(part, p, f), rs_buf.at[f, p], r_rsem.at[f]).start()
        drain(r_ssem.at[f], rs_buf.at[f, : plane - 1])
    to_plane(lambda q: kl_p.at[p], kl_p.at[p], kp_ssem, kp_rsem)
    drain(kp_ssem, kl_p.at[: plane - 1])

    arrived(h_rsem, hall)
    near = pl.ds(pl.multiple_of(half * 2 * rows, 2 * rows), 2 * rows)
    far = pl.ds(pl.multiple_of((1 - half) * 2 * rows, 2 * rows), 2 * rows)

    def outer(i, at):
        return lax.dot_general(
            hall[at, :], gall[i, at, :], (((0,), (0,)), ((), ())), preferred_element_type=F32
        )

    def got_core(i):
        arrived(g_rsem.at[0, i], gall.at[i, mine])

    def got_chip(i):
        arrived(g_rsem.at[1, i], gall.at[i, mine])
        g_pass(i).start()

    def got_pass(i):
        arrived(g_rsem.at[2, i], gall.at[i, mine])

    for i in range(4):
        got_core(i)
        acc[i] = outer(i, near)
    got_chip(0)
    got_chip(1)

    def r_sums(f):
        arrived(r_rsem.at[f], rs_buf.at[f])

        def add(q, total):
            return total + rs_buf[f, q].astype(F32)

        total = lax.fori_loop(0, plane, add, jnp.zeros((TB, fb_width), F32))
        z_send[f] = total.astype(BF16)
        z_copy(f).start()
        drain(z_ssem.at[f], z_send.at[f])

    def z_copy(f):
        return remote(z_send.at[f], z_recv.at[f], z_ssem.at[f], z_rsem.at[f], a, b_across)

    def spread(f):
        z_copy(f).wait_recv()
        fin[f] = (z_send[f].astype(F32) + z_recv[f].astype(F32)).astype(BF16)
        to_plane(lambda q: fin.at[f], block_of(gh_out, p, f), a_ssem.at[f], a_rsem.at[f])
        pltpu.make_async_copy(fin.at[f], block_of(gh_out, p, f), a_rsem.at[f]).start()
        drain(a_ssem.at[f], rs_buf.at[f, : plane - 1])

    r_sums(0)
    g_chip(3).start()
    got_chip(2)
    spread(0)
    r_sums(1)

    arrived(kp_rsem, kl_p.at[: plane - 1])
    kl_z[zh] = jnp.sum(kl_p[...], axis=0)
    kz_copy = remote(kl_z.at[zh], kl_z.at[zh], kz_ssem, kz_rsem, a, b_across)
    kz_copy.start()
    drain(kz_ssem, kl_z.at[zh])
    got_chip(3)
    spread(1)
    remote(kl_z.at[1 - zh], kl_z.at[1 - zh], kz_ssem, kz_rsem, a, b_across).wait_recv()
    kl_a[a] = jnp.sum(kl_z[...], axis=0)

    for step in range(1, 4):
        remote(kl_a.at[a], kl_a.at[a], ka_ssem, ka_rsem, (a + step) % 4, b).start()
    drain(ka_ssem, kl_a.at[:3])

    for i in range(4):
        got_pass(i)
        w_std[i, 0:share, :] = (acc[i] + outer(i, far)).astype(BF16)
    for k in range(share // sub):
        at = slice(k * sub, (k + 1) * sub)
        gw_out[at] = pltpu.einshape("idr->dir", w_std[:, at, :])
    arrived(ka_rsem, kl_a.at[:3])
    summed = jnp.sum(kl_a[...], axis=0)
    div_ref[...] = jnp.broadcast_to(
        jnp.sum(summed, axis=1, keepdims=True) / (4.0 * rows), div_ref.shape
    )
    half_width = width // HALVES
    for f in range(HALVES):
        arrived(a_rsem.at[f], gh_out.at[:, f * half_width : (f + 1) * half_width])
    finish(pending)


def store(div_in, gh_in, gw_in, div_ref, gh_hbm, gw_hbm, sem):
    n = gw_in.shape[0] // STORES
    copies = [
        pltpu.make_async_copy(
            gw_in.at[pl.ds(k * n, n)], gw_hbm.at[pl.ds(k * n, n)], sem.at[k]
        )
        for k in range(STORES)
    ]
    copies.append(pltpu.make_async_copy(gh_in, gh_hbm, sem.at[STORES]))
    for copy in copies:
        copy.start()
    div_ref[...] = div_in[0:1, 0:1]
    for copy in copies:
        copy.wait()


def on_device(n_ba, hidden, head_weight, teacher):
    rows, width = hidden.shape
    piece = head_weight.shape[3]
    share = width // 4
    plane = n_ba // 2
    per_a = n_ba // 4
    fb_width = width // (plane // per_a) // HALVES
    chunk = width // N_CHUNKS
    x_size = 4 if n_ba == 32 else 1
    dma = pltpu.SemaphoreType.DMA
    vmem, anywhere = pltpu.VMEM, pl.BlockSpec(memory_space=pl.ANY)
    results = pl.pallas_call(
        functools.partial(kernel, n_ba, x_size),
        out_shape=(
            vmem((8, 128), F32),
            vmem((rows, width), BF16),
            vmem((share, 4, piece), BF16),
        ),
        in_specs=[anywhere] * 3,
        out_specs=(pl.BlockSpec(memory_space=vmem),) * 3,
        scratch_shapes=[
            vmem((rows, width), BF16),
            vmem((N_CHUNKS, chunk, 4, piece), BF16),
            vmem((4, width, piece), BF16),
            vmem((4, piece, width), BF16),
            vmem((TB, n_ba, piece), BF16),
            vmem((n_ba, TB, piece), BF16),
            vmem((4, rows, piece), BF16),
            vmem((rows, 4 * piece), F32),
            vmem((n_ba, 1, rows), F32),
            vmem((1, rows), F32),
            vmem((4, per_a, 1, rows), F32),
            vmem((4 * rows, share), BF16),
            vmem((4, 4 * rows, piece), BF16),
            vmem((4, share, piece), F32),
            vmem((rows, width), BF16),
            vmem((HALVES, plane, TB, fb_width), BF16),
            vmem((HALVES, TB, fb_width), BF16),
            vmem((HALVES, TB, fb_width), BF16),
            vmem((HALVES, TB, fb_width), BF16),
            vmem((plane, 1, 128), F32),
            vmem((2, 1, 128), F32),
            vmem((4, 1, 128), F32),
            dma((2,)), dma((N_CHUNKS,)),
            dma, dma,
            dma, dma,
            dma, dma,
            dma, dma,
            dma((3,)), dma((3, 4)),
            dma((HALVES,)), dma((HALVES,)),
            dma((HALVES,)), dma((HALVES,)),
            dma((HALVES,)), dma((HALVES,)),
            dma, dma,
            dma, dma,
            dma, dma,
        ],
        compiler_params=pltpu.CompilerParams(
            collective_id=0, has_side_effects=True, vmem_limit_bytes=VMEM_LIMIT
        ),
    )(hidden, head_weight, teacher)
    div, grad_hidden, grad_head = pl.pallas_call(
        store,
        out_shape=(
            jax.ShapeDtypeStruct((1, 1), F32),
            jax.ShapeDtypeStruct((rows, width), BF16),
            jax.ShapeDtypeStruct((share, 4, piece), BF16),
        ),
        in_specs=[pl.BlockSpec(memory_space=vmem)] * 3,
        out_specs=(pl.BlockSpec(memory_space=vmem), anywhere, anywhere),
        scratch_shapes=[dma((STORES + 1,))],
        compiler_params=pltpu.CompilerParams(vmem_limit_bytes=1_000_000),
    )(*(pltpu.with_memory_space_constraint(x, vmem) for x in results))
    return div.reshape(()), grad_hidden, grad_head[:, None]


def solution(mesh):
    placed = (P("aa", None), P(None, "ba", None, None), P("ba", "aa", None, None))
    return jax.shard_map(
        functools.partial(on_device, mesh.shape["ba"]),
        mesh=mesh,
        in_specs=placed,
        out_specs=(P(), P("aa", None), P("aa", "ba", None, None)),
        check_vma=False,
    )
```

```python
import functools

import jax
import jax.numpy as jnp
from jax import lax
from jax.experimental import pallas as pl
from jax.experimental.pallas import tpu as pltpu
from jax.sharding import PartitionSpec as P

MESH = pl.DeviceIdType.MESH
F32 = jnp.float32
BF16 = jnp.bfloat16
grad_scale = 256.0
N_CHUNKS = 6
STORES = 6
HIDDEN_AT = 6
AHEAD = 3
LOADS_AFTER = 36
DIRECT = 2
TALK_AT = 1
ORDER = "c0,r0,h0,h1,h2,c1,r1,h3,s0,h4,h5"
ORDER_TAIL = "r2,p0,h6,s1,h7,m0,s2,q0,m1,c2,m2,c3,m3"
VMEM_LIMIT = 58_000_000
TB = 16
HALVES = 3


def finish(pending):
    for wait in pending:
        wait()


def ring(d, n):
    return min(d, n - d)


def offsets(y_size, x_size):
    steps = [(y, z, x) for y in range(y_size) for z in range(2) for x in range(x_size)]
    return sorted(steps, key=lambda s: -(ring(s[0], y_size) + 2 * s[1] + ring(s[2], x_size)))


def lanes_to_rows(row, n):
    return jnp.transpose(jnp.broadcast_to(row, (n, n)))


def kernel(
    n_ba, x_size,
    hid_hbm, w_hbm, t_hbm,
    div_ref, gh_out, gw_out,
    hid, w_raw, w_std, w_tr, t_raw, t_send, t_in, stu, lse_buf, n_send, n_in,
    hall, gall, acc, part, rs_buf, z_send, z_recv, fin, kl_p, kl_z, kl_a,
    in_sem, w_sem, t_ssem, t_rsem, n_ssem, n_rsem, h_ssem, h_rsem, s_ssem, s_rsem,
    g_ssem, g_rsem, r_ssem, r_rsem, z_ssem, z_rsem, a_ssem, a_rsem,
    kp_ssem, kp_rsem, kz_ssem, kz_rsem, ka_ssem, ka_rsem,
):
    a = lax.axis_index("aa")
    b = lax.axis_index("ba")
    width = hid.shape[1]
    rows = hid.shape[0]
    piece = w_raw.shape[3]
    per_a = n_ba // 4
    plane = n_ba // 2
    share = width // 4
    n_fb = plane // per_a
    fb_width = width // n_fb // HALVES
    chunk = w_raw.shape[1]
    t_owner = b // per_a
    t_slot = b % per_a
    y_size = n_ba // (2 * x_size)
    yy, zh, xx = b // (2 * x_size), (b // x_size) % 2, b % x_size
    p = yy * x_size + xx
    steps = offsets(y_size, x_size)
    plane_steps = [s for s in steps if s[1] == 0]

    def moved(step):
        y, z, x = step
        return (((yy + y) % y_size) * 2 + (zh + z) % 2) * x_size + (xx + x) % x_size

    half = a // 2

    def plane_peer(q):
        return ((q // x_size) * 2 + zh) * x_size + q % x_size

    b_across = plane_peer(p) + (1 - 2 * zh) * x_size
    core_mate = a + 1 - 2 * (a % 2)
    chip_mate = (a + 2) % 4

    def remote(src, dst, ssem, rsem, to_a, to_b):
        return pltpu.make_async_remote_copy(
            src_ref=src, dst_ref=dst, send_sem=ssem, recv_sem=rsem,
            device_id=(to_a, to_b), device_id_type=MESH,
        )

    pending = []

    def drain(sem, like):
        pending.append(remote(like, like, sem, sem, a, b).wait_send)

    def drain_t(sem, ref):
        def wait():
            @pl.when(t_owner == a)
            def _():
                remote(ref.at[: n_ba - 1], ref.at[: n_ba - 1], sem, sem, a, b).wait_send()

            @pl.when(t_owner != a)
            def _():
                remote(ref, ref, sem, sem, a, b).wait_send()

        pending.append(wait)

    t_load = pltpu.make_async_copy(t_hbm.at[:, 0], t_raw, in_sem.at[0])
    h_load = pltpu.make_async_copy(hid_hbm, hid, in_sem.at[1])
    t_load.start()

    def w_load(k):
        return pltpu.make_async_copy(
            w_hbm.at[pl.ds(k * chunk, chunk), 0], w_raw.at[k], w_sem.at[k]
        )

    barrier = pltpu.get_barrier_semaphore()

    def greet(to_a, to_b):
        pl.semaphore_signal(barrier, inc=1, device_id=(to_a, to_b), device_id_type=MESH)

    greetings = []
    for step in steps:
        hops = ring(step[0], y_size) + 2 * step[1] + ring(step[2], x_size)
        if hops:
            greetings.append((hops, 0, step))
    for da in range(4):
        for step in steps:
            if step[0] == 0:
                hops = ring(step[2], x_size) + (1 if da // 2 else 2 * step[1]) + 1
                greetings.append((hops, 1 + da, step))
    greetings.sort(key=lambda g: -g[0])

    def start_loads():
        h_load.start()
        for k in range(AHEAD):
            w_load(k).start()

    for n, (_, kind, step) in enumerate(greetings):
        if n == LOADS_AFTER:
            start_loads()
        if kind == 0:
            greet(a, moved(step))
            continue
        da = kind - 1
        src_a = ((half + da // 2) % 2) * 2 + (a + da) % 2
        src_b = (a * 2 + (zh + step[1]) % 2) * x_size + (xx + step[2]) % x_size
        if da or step != (0, 0, 0):
            greet(src_a, src_b)
        else:

            @pl.when(t_owner != a)
            def _():
                greet(src_a, src_b)

    b_near = moved((0, 1, 0))
    for step in range(1, 4):
        greet((a + step) % 4, b)
    for to_a in (chip_mate, 3 - a):
        greet(to_a, b_near)

    t_load.wait()
    t_send[...] = pltpu.einshape("tjr->jtr", t_raw[...])
    def t_max(j, m):
        return jnp.maximum(m, t_send[j].astype(F32))

    t_peak = lax.fori_loop(1, n_ba, t_max, t_send[0].astype(F32))
    t_peak = jnp.max(t_peak, axis=1, keepdims=True)

    def t_sum(j, s):
        return s + jnp.exp(t_send[j].astype(F32) - t_peak)

    t_total = lax.fori_loop(0, n_ba, t_sum, jnp.zeros((TB, piece), F32))
    t_lse = t_peak + jnp.log(jnp.sum(t_total, axis=1, keepdims=True))
    token = lax.broadcasted_iota(jnp.int32, (TB, rows), 0)
    lane = lax.broadcasted_iota(jnp.int32, (TB, rows), 1)
    n_send[...] = jnp.sum(
        jnp.where(lane == token + t_slot * TB, t_lse, 0.0), axis=0, keepdims=True
    )

    sub = chunk // 2

    def relayout(k, c):
        at = pl.ds(pl.multiple_of(k * sub, sub), sub)
        w_std[:, at, :] = pltpu.einshape(
            "dir->idr", w_raw[k // 2, pl.ds(pl.multiple_of((k % 2) * sub, sub), sub)]
        )
        return c

    t_dst = t_in.at[a, pl.ds(pl.multiple_of(t_slot * TB, TB), TB)]

    def to_owner(src_of, dst, ssem, rsem):
        for step in steps:
            k = moved(step)
            copy = remote(src_of(k), dst, ssem, rsem, t_owner, k)
            if step != (0, 0, 0):
                copy.start()
            else:

                @pl.when(t_owner != a)
                def _():
                    copy.start()

                @pl.when(t_owner == a)
                def _():
                    pltpu.make_async_copy(src_of(k), dst, rsem).start()

    def talk():
        expected = 2 * n_ba - 1 + 5 - jnp.where(t_owner == a, 1, 0)
        pl.semaphore_wait(barrier, expected)
        to_owner(lambda k: t_send.at[k], t_dst, t_ssem, t_rsem)
        to_owner(lambda k: n_send, n_in.at[a, t_slot], n_ssem, n_rsem)

    drain_t(t_ssem, t_send)
    drain_t(n_ssem, lse_buf)
    pl.when(zh != 0)(talk)
    h_load.wait()
    for part_of in range(2):
        if part_of == TALK_AT:
            pl.when(zh == 0)(talk)
        for k in range(part_of * N_CHUNKS // 2, (part_of + 1) * N_CHUNKS // 2):
            w_load(k).wait()
            if k + AHEAD < N_CHUNKS:
                w_load(k + AHEAD).start()
            lax.fori_loop(2 * k, 2 * k + 2, relayout, 0)
        deep = slice(part_of * width // 2, (part_of + 1) * width // 2)
        for i in range(4):
            at = slice(i * piece, (i + 1) * piece)
            product = jnp.dot(hid[:, deep], w_std[i, deep], preferred_element_type=F32)
            stu[:, at] = product if part_of == 0 else stu[:, at] + product
    s = stu[...]
    s_peak = jnp.max(s, axis=1, keepdims=True)
    s_total = jnp.sum(jnp.exp(s - s_peak), axis=1, keepdims=True)
    s_part = s_peak + jnp.log(s_total)
    lse_buf[b] = jnp.transpose(jnp.broadcast_to(s_part, (rows, rows)))[0:1, :]

    for step in steps[:-1]:
        remote(lse_buf.at[b], lse_buf.at[b], s_ssem, s_rsem, a, moved(step)).start()
    drain(s_ssem, lse_buf.at[: n_ba - 1])

    mine = pl.ds(pl.multiple_of(a * rows, rows), rows)

    def h_part(to_a, to_b, start, size):
        src = hid_hbm.at[pl.ds(start, size), pl.ds(pl.multiple_of(to_a * share, share), share)]
        dst = hall.at[pl.ds(pl.multiple_of(a * rows + start, size), size)]
        return remote(src, dst, h_ssem, h_rsem, to_a, to_b)

    def send_hidden():
        for to_a in (chip_mate, 3 - a):
            h_part(to_a, b, 0, rows // 2).start()
            h_part(to_a, b_near, rows // 2, rows // 2).start()
        h_part(core_mate, b, 0, rows).start()
        own = hid_hbm.at[:, pl.ds(pl.multiple_of(a * share, share), share)]
        pltpu.make_async_copy(own, hall.at[mine], h_rsem).start()

    drain(h_ssem, hall.at[: 3 * rows])

    def turn(k, c):
        at = pl.ds(pl.multiple_of(k * sub, sub), sub)
        for i in range(4):
            w_tr[i, :, at] = jnp.transpose(w_std[i, at, :])
        return c

    lax.fori_loop(0, HIDDEN_AT, turn, 0)
    send_hidden()
    lax.fori_loop(HIDDEN_AT, 2 * N_CHUNKS, turn, 0)

    def arrived(sem, like):
        remote(like, like, sem, sem, a, b).wait_recv()

    arrived(s_rsem, lse_buf.at[: n_ba - 1])
    parts = lse_buf[...]
    s_top = jnp.max(parts, axis=0)
    s_lse = s_top + jnp.log(jnp.sum(jnp.exp(parts - s_top[None]), axis=0))
    s_lse = lanes_to_rows(s_lse, rows)[:, 0:1]

    arrived(t_rsem, t_in)
    arrived(n_rsem, n_in)
    t_parts = jnp.sum(n_in[...], axis=1)
    t_top = jnp.max(t_parts, axis=0)
    t_all = t_top + jnp.log(jnp.sum(jnp.exp(t_parts - t_top[None]), axis=0))
    t_all = lanes_to_rows(t_all, rows)[:, 0:1]

    def g_copy(i, src_a, to_a, ssem, rsem):
        at = pl.ds(pl.multiple_of(src_a * rows, rows), rows)
        return remote(gall.at[i, at], gall.at[i, at], ssem, rsem, to_a, b)

    def g_core(i):
        return g_copy(i, a, core_mate, g_ssem.at[0], g_rsem.at[0, i])

    def g_chip(i):
        return g_copy(i, a, chip_mate, g_ssem.at[1], g_rsem.at[1, i])

    def g_late(n):
        i, k = DIRECT + n // 4, n % 4
        at = pl.ds(pl.multiple_of(a * rows + k * (rows // 4), rows // 4), rows // 4)
        remote(gall.at[i, at], gall.at[i, at], g_ssem.at[1], g_rsem.at[1, i], chip_mate, b).start()

    def g_pass(i):
        return g_copy(i, chip_mate, core_mate, g_ssem.at[2], g_rsem.at[2, i])

    for k in range(3):
        drain(g_ssem.at[k], gall.at[:, mine])

    kl = jnp.zeros((rows, 128), F32)
    for i in range(4):
        log_target = t_in[i].astype(F32) - t_all
        log_student = stu[:, i * piece : (i + 1) * piece] - s_lse
        target_prob = jnp.exp(log_target)
        student_prob = jnp.exp(log_student)
        gall[i, mine, :] = (grad_scale * (student_prob - target_prob)).astype(BF16)
        term = target_prob * (log_target - log_student)
        for v in range(piece // 128):
            kl = kl + term[:, v * 128 : (v + 1) * 128]
        if i > 0:
            if i <= DIRECT:
                g_chip(i - 1).start()
            g_core(i - 1).start()
    kl_p[p] = jnp.sum(kl, axis=0, keepdims=True)
    g_core(3).start()

    def block_of(ref, q, f):
        return ref.at[
            pl.ds(pl.multiple_of((q % per_a) * TB, TB), TB),
            pl.ds(pl.multiple_of((f * n_fb + q // per_a) * fb_width, fb_width), fb_width),
        ]

    def to_plane(src_of, dst, ssem, rsem):
        for step in plane_steps[:-1]:
            q = ((yy + step[0]) % y_size) * x_size + (xx + step[2]) % x_size
            remote(src_of(q), dst, ssem, rsem, a, moved(step)).start()

    for f in range(HALVES):
        cols = slice(f * n_fb * fb_width, (f + 1) * n_fb * fb_width)
        total = None
        for i in range(4):
            term = jnp.dot(gall[i, mine, :], w_tr[i, :, cols], preferred_element_type=F32)
            total = term if total is None else total + term
        part[:, cols] = total.astype(BF16)
        to_plane(lambda q: block_of(part, q, f), rs_buf.at[f, p], r_ssem.at[f], r_rsem.at[f])
        pltpu.make_async_copy(block_of(part, p, f), rs_buf.at[f, p], r_rsem.at[f]).start()
        drain(r_ssem.at[f], rs_buf.at[f, : plane - 1])
    to_plane(lambda q: kl_p.at[p], kl_p.at[p], kp_ssem, kp_rsem)
    drain(kp_ssem, kl_p.at[: plane - 1])

    arrived(h_rsem, hall)
    near = pl.ds(pl.multiple_of(half * 2 * rows, 2 * rows), 2 * rows)
    far = pl.ds(pl.multiple_of((1 - half) * 2 * rows, 2 * rows), 2 * rows)

    def outer(i, at):
        return lax.dot_general(
            hall[at, :], gall[i, at, :], (((0,), (0,)), ((), ())), preferred_element_type=F32
        )

    def got_core(i):
        arrived(g_rsem.at[0, i], gall.at[i, mine])

    def got_chip(i):
        arrived(g_rsem.at[1, i], gall.at[i, mine])
        g_pass(i).start()

    def got_pass(i):
        arrived(g_rsem.at[2, i], gall.at[i, mine])

    for i in range(4):
        got_core(i)
        acc[i] = outer(i, near)
    def r_sums(f):
        arrived(r_rsem.at[f], rs_buf.at[f])

        def add(q, total):
            return total + rs_buf[f, q].astype(F32)

        total = lax.fori_loop(0, plane, add, jnp.zeros((TB, fb_width), F32))
        z_send[f] = total.astype(BF16)
        z_copy(f).start()
        drain(z_ssem.at[f], z_send.at[f])

    def z_copy(f):
        return remote(z_send.at[f], z_recv.at[f], z_ssem.at[f], z_rsem.at[f], a, b_across)

    def spread(f):
        z_copy(f).wait_recv()
        fin[f] = (z_send[f].astype(F32) + z_recv[f].astype(F32)).astype(BF16)
        to_plane(lambda q: fin.at[f], block_of(gh_out, p, f), a_ssem.at[f], a_rsem.at[f])
        pltpu.make_async_copy(fin.at[f], block_of(gh_out, p, f), a_rsem.at[f]).start()
        drain(a_ssem.at[f], rs_buf.at[f, : plane - 1])

    def kz_of(zz):
        return remote(kl_z.at[zz], kl_z.at[zz], kz_ssem, kz_rsem, a, b_across)

    def loss_plane(_):
        arrived(kp_rsem, kl_p.at[: plane - 1])
        kl_z[zh] = jnp.sum(kl_p[...], axis=0)
        kz_of(zh).start()

    def loss_across(_):
        kz_of(1 - zh).wait_recv()
        kl_a[a] = jnp.sum(kl_z[...], axis=0)
        for step in range(1, 4):
            remote(kl_a.at[a], kl_a.at[a], ka_ssem, ka_rsem, (a + step) % 4, b).start()

    drain(kz_ssem, kl_z.at[zh])
    drain(ka_ssem, kl_a.at[:3])

    def far_tokens(i):
        got_pass(i)
        w_std[i, 0:share, :] = (acc[i] + outer(i, far)).astype(BF16)

    for event in (ORDER + "," + ORDER_TAIL).split(","):
        {"c": got_chip, "r": r_sums, "s": spread, "h": g_late, "m": far_tokens,
            "p": loss_plane, "q": loss_across}[event[0]](
            int(event[1])
        )
    for k in range(share // sub):
        at = slice(k * sub, (k + 1) * sub)
        gw_out[at] = pltpu.einshape("idr->dir", w_std[:, at, :])
    arrived(ka_rsem, kl_a.at[:3])
    summed = jnp.sum(kl_a[...], axis=0)
    div_ref[...] = jnp.broadcast_to(
        jnp.sum(summed, axis=1, keepdims=True) / (4.0 * rows), div_ref.shape
    )
    half_width = width // HALVES
    for f in range(HALVES):
        arrived(a_rsem.at[f], gh_out.at[:, f * half_width : (f + 1) * half_width])
    finish(pending)


def store(div_in, gh_in, gw_in, div_ref, gh_hbm, gw_hbm, sem):
    n = gw_in.shape[0] // STORES
    copies = [
        pltpu.make_async_copy(
            gw_in.at[pl.ds(k * n, n)], gw_hbm.at[pl.ds(k * n, n)], sem.at[k]
        )
        for k in range(STORES)
    ]
    copies.append(pltpu.make_async_copy(gh_in, gh_hbm, sem.at[STORES]))
    for copy in copies:
        copy.start()
    div_ref[...] = div_in[0:1, 0:1]
    for copy in copies:
        copy.wait()


def on_device(n_ba, hidden, head_weight, teacher):
    rows, width = hidden.shape
    piece = head_weight.shape[3]
    share = width // 4
    plane = n_ba // 2
    per_a = n_ba // 4
    fb_width = width // (plane // per_a) // HALVES
    chunk = width // N_CHUNKS
    x_size = 4 if n_ba == 32 else 1
    dma = pltpu.SemaphoreType.DMA
    vmem, anywhere = pltpu.VMEM, pl.BlockSpec(memory_space=pl.ANY)
    results = pl.pallas_call(
        functools.partial(kernel, n_ba, x_size),
        out_shape=(
            vmem((8, 128), F32),
            vmem((rows, width), BF16),
            vmem((share, 4, piece), BF16),
        ),
        in_specs=[anywhere] * 3,
        out_specs=(pl.BlockSpec(memory_space=vmem),) * 3,
        scratch_shapes=[
            vmem((rows, width), BF16),
            vmem((N_CHUNKS, chunk, 4, piece), BF16),
            vmem((4, width, piece), BF16),
            vmem((4, piece, width), BF16),
            vmem((TB, n_ba, piece), BF16),
            vmem((n_ba, TB, piece), BF16),
            vmem((4, rows, piece), BF16),
            vmem((rows, 4 * piece), F32),
            vmem((n_ba, 1, rows), F32),
            vmem((1, rows), F32),
            vmem((4, per_a, 1, rows), F32),
            vmem((4 * rows, share), BF16),
            vmem((4, 4 * rows, piece), BF16),
            vmem((4, share, piece), F32),
            vmem((rows, width), BF16),
            vmem((HALVES, plane, TB, fb_width), BF16),
            vmem((HALVES, TB, fb_width), BF16),
            vmem((HALVES, TB, fb_width), BF16),
            vmem((HALVES, TB, fb_width), BF16),
            vmem((plane, 1, 128), F32),
            vmem((2, 1, 128), F32),
            vmem((4, 1, 128), F32),
            dma((2,)), dma((N_CHUNKS,)),
            dma, dma,
            dma, dma,
            dma, dma,
            dma, dma,
            dma((3,)), dma((3, 4)),
            dma((HALVES,)), dma((HALVES,)),
            dma((HALVES,)), dma((HALVES,)),
            dma((HALVES,)), dma((HALVES,)),
            dma, dma,
            dma, dma,
            dma, dma,
        ],
        compiler_params=pltpu.CompilerParams(
            collective_id=0, has_side_effects=True, vmem_limit_bytes=VMEM_LIMIT
        ),
    )(hidden, head_weight, teacher)
    div, grad_hidden, grad_head = pl.pallas_call(
        store,
        out_shape=(
            jax.ShapeDtypeStruct((1, 1), F32),
            jax.ShapeDtypeStruct((rows, width), BF16),
            jax.ShapeDtypeStruct((share, 4, piece), BF16),
        ),
        in_specs=[pl.BlockSpec(memory_space=vmem)] * 3,
        out_specs=(pl.BlockSpec(memory_space=vmem), anywhere, anywhere),
        scratch_shapes=[dma((STORES + 1,))],
        compiler_params=pltpu.CompilerParams(vmem_limit_bytes=1_000_000),
    )(*(pltpu.with_memory_space_constraint(x, vmem) for x in results))
    return div.reshape(()), grad_hidden, grad_head[:, None]


def solution(mesh):
    placed = (P("aa", None), P(None, "ba", None, None), P("ba", "aa", None, None))
    return jax.shard_map(
        functools.partial(on_device, mesh.shape["ba"]),
        mesh=mesh,
        in_specs=placed,
        out_specs=(P(), P("aa", None), P("aa", "ba", None, None)),
        check_vma=False,
    )
```

```python
import functools

import jax
import jax.numpy as jnp
from jax import lax
from jax.experimental import pallas as pl
from jax.experimental.pallas import tpu as pltpu
from jax.sharding import PartitionSpec as P

MESH = pl.DeviceIdType.MESH
F32 = jnp.float32
BF16 = jnp.bfloat16
grad_scale = 256.0
N_CHUNKS = 6
STORES = 6
HIDDEN_AT = 6
AHEAD = 3
LOADS_AFTER = 36
DIRECT = 2
TALK_AT = 1
ORDER = "c0,r0,h0,h1,h2,c1,r1,h3,s0,h4,h5"
ORDER_TAIL = "r2,p0,h6,s1,h7,c2,m0,s2,q0,m1,m2,c3,m3"
VMEM_LIMIT = 58_000_000
TB = 16
HALVES = 3


def finish(pending):
    for wait in pending:
        wait()


def ring(d, n):
    return min(d, n - d)


def offsets(y_size, x_size):
    steps = [(y, z, x) for y in range(y_size) for z in range(2) for x in range(x_size)]
    return sorted(steps, key=lambda s: -(ring(s[0], y_size) + 2 * s[1] + ring(s[2], x_size)))


def lanes_to_rows(row, n):
    return jnp.transpose(jnp.broadcast_to(row, (n, n)))


def kernel(
    n_ba, x_size,
    hid_hbm, w_hbm, t_hbm,
    div_ref, gh_out, gw_out,
    hid, w_raw, w_std, w_tr, t_raw, t_send, t_in, stu, lse_buf, n_send, n_in,
    hall, gall, acc, part, rs_buf, z_send, z_recv, fin, kl_p, kl_z, kl_a,
    in_sem, w_sem, t_ssem, t_rsem, n_ssem, n_rsem, h_ssem, h_rsem, s_ssem, s_rsem,
    g_ssem, g_rsem, r_ssem, r_rsem, z_ssem, z_rsem, a_ssem, a_rsem,
    kp_ssem, kp_rsem, kz_ssem, kz_rsem, ka_ssem, ka_rsem,
):
    a = lax.axis_index("aa")
    b = lax.axis_index("ba")
    width = hid.shape[1]
    rows = hid.shape[0]
    piece = w_raw.shape[3]
    per_a = n_ba // 4
    plane = n_ba // 2
    share = width // 4
    n_fb = plane // per_a
    fb_width = width // n_fb // HALVES
    chunk = w_raw.shape[1]
    t_owner = b // per_a
    t_slot = b % per_a
    y_size = n_ba // (2 * x_size)
    yy, zh, xx = b // (2 * x_size), (b // x_size) % 2, b % x_size
    p = yy * x_size + xx
    steps = offsets(y_size, x_size)
    plane_steps = [s for s in steps if s[1] == 0]

    def moved(step):
        y, z, x = step
        return (((yy + y) % y_size) * 2 + (zh + z) % 2) * x_size + (xx + x) % x_size

    half = a // 2

    def plane_peer(q):
        return ((q // x_size) * 2 + zh) * x_size + q % x_size

    b_across = plane_peer(p) + (1 - 2 * zh) * x_size
    core_mate = a + 1 - 2 * (a % 2)
    chip_mate = (a + 2) % 4

    def remote(src, dst, ssem, rsem, to_a, to_b):
        return pltpu.make_async_remote_copy(
            src_ref=src, dst_ref=dst, send_sem=ssem, recv_sem=rsem,
            device_id=(to_a, to_b), device_id_type=MESH,
        )

    pending = []

    def drain(sem, like):
        pending.append(remote(like, like, sem, sem, a, b).wait_send)

    def drain_t(sem, ref):
        def wait():
            @pl.when(t_owner == a)
            def _():
                remote(ref.at[: n_ba - 1], ref.at[: n_ba - 1], sem, sem, a, b).wait_send()

            @pl.when(t_owner != a)
            def _():
                remote(ref, ref, sem, sem, a, b).wait_send()

        pending.append(wait)

    t_load = pltpu.make_async_copy(t_hbm.at[:, 0], t_raw, in_sem.at[0])
    h_load = pltpu.make_async_copy(hid_hbm, hid, in_sem.at[1])
    t_load.start()

    def w_load(k):
        return pltpu.make_async_copy(
            w_hbm.at[pl.ds(k * chunk, chunk), 0], w_raw.at[k], w_sem.at[k]
        )

    barrier = pltpu.get_barrier_semaphore()

    def greet(to_a, to_b):
        pl.semaphore_signal(barrier, inc=1, device_id=(to_a, to_b), device_id_type=MESH)

    greetings = []
    for step in steps:
        hops = ring(step[0], y_size) + 2 * step[1] + ring(step[2], x_size)
        if hops:
            greetings.append((hops, 0, step))
    for da in range(4):
        for step in steps:
            if step[0] == 0:
                hops = ring(step[2], x_size) + (1 if da // 2 else 2 * step[1]) + 1
                greetings.append((hops, 1 + da, step))
    greetings.sort(key=lambda g: -g[0])

    def start_loads():
        h_load.start()
        for k in range(AHEAD):
            w_load(k).start()

    for n, (_, kind, step) in enumerate(greetings):
        if n == LOADS_AFTER:
            start_loads()
        if kind == 0:
            greet(a, moved(step))
            continue
        da = kind - 1
        src_a = ((half + da // 2) % 2) * 2 + (a + da) % 2
        src_b = (a * 2 + (zh + step[1]) % 2) * x_size + (xx + step[2]) % x_size
        if da or step != (0, 0, 0):
            greet(src_a, src_b)
        else:

            @pl.when(t_owner != a)
            def _():
                greet(src_a, src_b)

    b_near = moved((0, 1, 0))
    for step in range(1, 4):
        greet((a + step) % 4, b)
    for to_a in (chip_mate, 3 - a):
        greet(to_a, b_near)

    t_load.wait()
    t_send[...] = pltpu.einshape("tjr->jtr", t_raw[...])
    def t_max(j, m):
        return jnp.maximum(m, t_send[j].astype(F32))

    t_peak = lax.fori_loop(1, n_ba, t_max, t_send[0].astype(F32))
    t_peak = jnp.max(t_peak, axis=1, keepdims=True)

    def t_sum(j, s):
        return s + jnp.exp(t_send[j].astype(F32) - t_peak)

    t_total = lax.fori_loop(0, n_ba, t_sum, jnp.zeros((TB, piece), F32))
    t_lse = t_peak + jnp.log(jnp.sum(t_total, axis=1, keepdims=True))
    token = lax.broadcasted_iota(jnp.int32, (TB, rows), 0)
    lane = lax.broadcasted_iota(jnp.int32, (TB, rows), 1)
    n_send[...] = jnp.sum(
        jnp.where(lane == token + t_slot * TB, t_lse, 0.0), axis=0, keepdims=True
    )

    sub = chunk // 2

    def relayout(k, c):
        at = pl.ds(pl.multiple_of(k * sub, sub), sub)
        w_std[:, at, :] = pltpu.einshape(
            "dir->idr", w_raw[k // 2, pl.ds(pl.multiple_of((k % 2) * sub, sub), sub)]
        )
        return c

    t_dst = t_in.at[a, pl.ds(pl.multiple_of(t_slot * TB, TB), TB)]

    def to_owner(src_of, dst, ssem, rsem):
        for step in steps:
            k = moved(step)
            copy = remote(src_of(k), dst, ssem, rsem, t_owner, k)
            if step != (0, 0, 0):
                copy.start()
            else:

                @pl.when(t_owner != a)
                def _():
                    copy.start()

                @pl.when(t_owner == a)
                def _():
                    pltpu.make_async_copy(src_of(k), dst, rsem).start()

    def talk():
        expected = 2 * n_ba - 1 + 5 - jnp.where(t_owner == a, 1, 0)
        pl.semaphore_wait(barrier, expected)
        to_owner(lambda k: t_send.at[k], t_dst, t_ssem, t_rsem)
        to_owner(lambda k: n_send, n_in.at[a, t_slot], n_ssem, n_rsem)

    drain_t(t_ssem, t_send)
    drain_t(n_ssem, lse_buf)
    pl.when(zh != 0)(talk)
    h_load.wait()
    for part_of in range(2):
        if part_of == TALK_AT:
            pl.when(zh == 0)(talk)
        for k in range(part_of * N_CHUNKS // 2, (part_of + 1) * N_CHUNKS // 2):
            w_load(k).wait()
            if k + AHEAD < N_CHUNKS:
                w_load(k + AHEAD).start()
            lax.fori_loop(2 * k, 2 * k + 2, relayout, 0)
        deep = slice(part_of * width // 2, (part_of + 1) * width // 2)
        for i in range(4):
            at = slice(i * piece, (i + 1) * piece)
            product = jnp.dot(hid[:, deep], w_std[i, deep], preferred_element_type=F32)
            stu[:, at] = product if part_of == 0 else stu[:, at] + product
    s = stu[...]
    s_peak = jnp.max(s, axis=1, keepdims=True)
    s_total = jnp.sum(jnp.exp(s - s_peak), axis=1, keepdims=True)
    s_part = s_peak + jnp.log(s_total)
    lse_buf[b] = jnp.transpose(jnp.broadcast_to(s_part, (rows, rows)))[0:1, :]

    for step in steps[:-1]:
        remote(lse_buf.at[b], lse_buf.at[b], s_ssem, s_rsem, a, moved(step)).start()
    drain(s_ssem, lse_buf.at[: n_ba - 1])

    mine = pl.ds(pl.multiple_of(a * rows, rows), rows)

    def h_part(to_a, to_b, start, size):
        src = hid_hbm.at[pl.ds(start, size), pl.ds(pl.multiple_of(to_a * share, share), share)]
        dst = hall.at[pl.ds(pl.multiple_of(a * rows + start, size), size)]
        return remote(src, dst, h_ssem, h_rsem, to_a, to_b)

    def send_hidden():
        for to_a in (chip_mate, 3 - a):
            h_part(to_a, b, 0, rows // 2).start()
            h_part(to_a, b_near, rows // 2, rows // 2).start()
        h_part(core_mate, b, 0, rows).start()
        own = hid_hbm.at[:, pl.ds(pl.multiple_of(a * share, share), share)]
        pltpu.make_async_copy(own, hall.at[mine], h_rsem).start()

    drain(h_ssem, hall.at[: 3 * rows])

    def turn(k, c):
        at = pl.ds(pl.multiple_of(k * sub, sub), sub)
        for i in range(4):
            w_tr[i, :, at] = jnp.transpose(w_std[i, at, :])
        return c

    lax.fori_loop(0, HIDDEN_AT, turn, 0)
    send_hidden()
    lax.fori_loop(HIDDEN_AT, 2 * N_CHUNKS, turn, 0)

    def arrived(sem, like):
        remote(like, like, sem, sem, a, b).wait_recv()

    arrived(s_rsem, lse_buf.at[: n_ba - 1])
    parts = lse_buf[...]
    s_top = jnp.max(parts, axis=0)
    s_lse = s_top + jnp.log(jnp.sum(jnp.exp(parts - s_top[None]), axis=0))
    s_lse = lanes_to_rows(s_lse, rows)[:, 0:1]

    arrived(t_rsem, t_in)
    arrived(n_rsem, n_in)
    t_parts = jnp.sum(n_in[...], axis=1)
    t_top = jnp.max(t_parts, axis=0)
    t_all = t_top + jnp.log(jnp.sum(jnp.exp(t_parts - t_top[None]), axis=0))
    t_all = lanes_to_rows(t_all, rows)[:, 0:1]

    def g_copy(i, src_a, to_a, ssem, rsem):
        at = pl.ds(pl.multiple_of(src_a * rows, rows), rows)
        return remote(gall.at[i, at], gall.at[i, at], ssem, rsem, to_a, b)

    def g_core(i):
        return g_copy(i, a, core_mate, g_ssem.at[0], g_rsem.at[0, i])

    def g_chip(i):
        return g_copy(i, a, chip_mate, g_ssem.at[1], g_rsem.at[1, i])

    def g_late(n):
        i, k = DIRECT + n // 4, n % 4
        at = pl.ds(pl.multiple_of(a * rows + k * (rows // 4), rows // 4), rows // 4)
        remote(gall.at[i, at], gall.at[i, at], g_ssem.at[1], g_rsem.at[1, i], chip_mate, b).start()

    def g_pass(i):
        return g_copy(i, chip_mate, core_mate, g_ssem.at[2], g_rsem.at[2, i])

    for k in range(3):
        drain(g_ssem.at[k], gall.at[:, mine])

    kl = jnp.zeros((rows, 128), F32)
    for i in range(4):
        log_target = t_in[i].astype(F32) - t_all
        log_student = stu[:, i * piece : (i + 1) * piece] - s_lse
        target_prob = jnp.exp(log_target)
        student_prob = jnp.exp(log_student)
        gall[i, mine, :] = (grad_scale * (student_prob - target_prob)).astype(BF16)
        term = target_prob * (log_target - log_student)
        for v in range(piece // 128):
            kl = kl + term[:, v * 128 : (v + 1) * 128]
        if i > 0:
            if i <= DIRECT:
                g_chip(i - 1).start()
            g_core(i - 1).start()
    kl_p[p] = jnp.sum(kl, axis=0, keepdims=True)
    g_core(3).start()

    def block_of(ref, q, f):
        return ref.at[
            pl.ds(pl.multiple_of((q % per_a) * TB, TB), TB),
            pl.ds(pl.multiple_of((f * n_fb + q // per_a) * fb_width, fb_width), fb_width),
        ]

    def to_plane(src_of, dst, ssem, rsem):
        for step in plane_steps[:-1]:
            q = ((yy + step[0]) % y_size) * x_size + (xx + step[2]) % x_size
            remote(src_of(q), dst, ssem, rsem, a, moved(step)).start()

    for f in range(HALVES):
        cols = slice(f * n_fb * fb_width, (f + 1) * n_fb * fb_width)
        total = None
        for i in range(4):
            term = jnp.dot(gall[i, mine, :], w_tr[i, :, cols], preferred_element_type=F32)
            total = term if total is None else total + term
        part[:, cols] = total.astype(BF16)
        to_plane(lambda q: block_of(part, q, f), rs_buf.at[f, p], r_ssem.at[f], r_rsem.at[f])
        pltpu.make_async_copy(block_of(part, p, f), rs_buf.at[f, p], r_rsem.at[f]).start()
        drain(r_ssem.at[f], rs_buf.at[f, : plane - 1])
    to_plane(lambda q: kl_p.at[p], kl_p.at[p], kp_ssem, kp_rsem)
    drain(kp_ssem, kl_p.at[: plane - 1])

    arrived(h_rsem, hall)
    near = pl.ds(pl.multiple_of(half * 2 * rows, 2 * rows), 2 * rows)
    far = pl.ds(pl.multiple_of((1 - half) * 2 * rows, 2 * rows), 2 * rows)

    def outer(i, at):
        return lax.dot_general(
            hall[at, :], gall[i, at, :], (((0,), (0,)), ((), ())), preferred_element_type=F32
        )

    def got_core(i):
        arrived(g_rsem.at[0, i], gall.at[i, mine])

    def got_chip(i):
        arrived(g_rsem.at[1, i], gall.at[i, mine])
        g_pass(i).start()

    def got_pass(i):
        arrived(g_rsem.at[2, i], gall.at[i, mine])

    for i in range(4):
        got_core(i)
        acc[i] = outer(i, near)
    def r_sums(f):
        arrived(r_rsem.at[f], rs_buf.at[f])

        def add(q, total):
            return total + rs_buf[f, q].astype(F32)

        total = lax.fori_loop(0, plane, add, jnp.zeros((TB, fb_width), F32))
        z_send[f] = total.astype(BF16)
        z_copy(f).start()
        drain(z_ssem.at[f], z_send.at[f])

    def z_copy(f):
        return remote(z_send.at[f], z_recv.at[f], z_ssem.at[f], z_rsem.at[f], a, b_across)

    def spread(f):
        z_copy(f).wait_recv()
        fin[f] = (z_send[f].astype(F32) + z_recv[f].astype(F32)).astype(BF16)
        to_plane(lambda q: fin.at[f], block_of(gh_out, p, f), a_ssem.at[f], a_rsem.at[f])
        pltpu.make_async_copy(fin.at[f], block_of(gh_out, p, f), a_rsem.at[f]).start()
        drain(a_ssem.at[f], rs_buf.at[f, : plane - 1])

    def kz_of(zz):
        return remote(kl_z.at[zz], kl_z.at[zz], kz_ssem, kz_rsem, a, b_across)

    def loss_plane(_):
        arrived(kp_rsem, kl_p.at[: plane - 1])
        kl_z[zh] = jnp.sum(kl_p[...], axis=0)
        kz_of(zh).start()

    def loss_across(_):
        kz_of(1 - zh).wait_recv()
        kl_a[a] = jnp.sum(kl_z[...], axis=0)
        for step in range(1, 4):
            remote(kl_a.at[a], kl_a.at[a], ka_ssem, ka_rsem, (a + step) % 4, b).start()

    drain(kz_ssem, kl_z.at[zh])
    drain(ka_ssem, kl_a.at[:3])

    def far_tokens(i):
        got_pass(i)
        w_std[i, 0:share, :] = (acc[i] + outer(i, far)).astype(BF16)

    for event in (ORDER + "," + ORDER_TAIL).split(","):
        {"c": got_chip, "r": r_sums, "s": spread, "h": g_late, "m": far_tokens,
            "p": loss_plane, "q": loss_across}[event[0]](
            int(event[1])
        )
    for k in range(share // sub):
        at = slice(k * sub, (k + 1) * sub)
        gw_out[at] = pltpu.einshape("idr->dir", w_std[:, at, :])
    arrived(ka_rsem, kl_a.at[:3])
    summed = jnp.sum(kl_a[...], axis=0)
    div_ref[...] = jnp.broadcast_to(
        jnp.sum(summed, axis=1, keepdims=True) / (4.0 * rows), div_ref.shape
    )
    half_width = width // HALVES
    for f in range(HALVES):
        arrived(a_rsem.at[f], gh_out.at[:, f * half_width : (f + 1) * half_width])
    finish(pending)


def store(div_in, gh_in, gw_in, div_ref, gh_hbm, gw_hbm, sem):
    n = gw_in.shape[0] // STORES
    copies = [
        pltpu.make_async_copy(
            gw_in.at[pl.ds(k * n, n)], gw_hbm.at[pl.ds(k * n, n)], sem.at[k]
        )
        for k in range(STORES)
    ]
    copies.append(pltpu.make_async_copy(gh_in, gh_hbm, sem.at[STORES]))
    for copy in copies:
        copy.start()
    div_ref[...] = div_in[0:1, 0:1]
    for copy in copies:
        copy.wait()


def on_device(n_ba, hidden, head_weight, teacher):
    rows, width = hidden.shape
    piece = head_weight.shape[3]
    share = width // 4
    plane = n_ba // 2
    per_a = n_ba // 4
    fb_width = width // (plane // per_a) // HALVES
    chunk = width // N_CHUNKS
    x_size = 4 if n_ba == 32 else 1
    dma = pltpu.SemaphoreType.DMA
    vmem, anywhere = pltpu.VMEM, pl.BlockSpec(memory_space=pl.ANY)
    results = pl.pallas_call(
        functools.partial(kernel, n_ba, x_size),
        out_shape=(
            vmem((8, 128), F32),
            vmem((rows, width), BF16),
            vmem((share, 4, piece), BF16),
        ),
        in_specs=[anywhere] * 3,
        out_specs=(pl.BlockSpec(memory_space=vmem),) * 3,
        scratch_shapes=[
            vmem((rows, width), BF16),
            vmem((N_CHUNKS, chunk, 4, piece), BF16),
            vmem((4, width, piece), BF16),
            vmem((4, piece, width), BF16),
            vmem((TB, n_ba, piece), BF16),
            vmem((n_ba, TB, piece), BF16),
            vmem((4, rows, piece), BF16),
            vmem((rows, 4 * piece), F32),
            vmem((n_ba, 1, rows), F32),
            vmem((1, rows), F32),
            vmem((4, per_a, 1, rows), F32),
            vmem((4 * rows, share), BF16),
            vmem((4, 4 * rows, piece), BF16),
            vmem((4, share, piece), F32),
            vmem((rows, width), BF16),
            vmem((HALVES, plane, TB, fb_width), BF16),
            vmem((HALVES, TB, fb_width), BF16),
            vmem((HALVES, TB, fb_width), BF16),
            vmem((HALVES, TB, fb_width), BF16),
            vmem((plane, 1, 128), F32),
            vmem((2, 1, 128), F32),
            vmem((4, 1, 128), F32),
            dma((2,)), dma((N_CHUNKS,)),
            dma, dma,
            dma, dma,
            dma, dma,
            dma, dma,
            dma((3,)), dma((3, 4)),
            dma((HALVES,)), dma((HALVES,)),
            dma((HALVES,)), dma((HALVES,)),
            dma((HALVES,)), dma((HALVES,)),
            dma, dma,
            dma, dma,
            dma, dma,
        ],
        compiler_params=pltpu.CompilerParams(
            collective_id=0, has_side_effects=True, vmem_limit_bytes=VMEM_LIMIT
        ),
    )(hidden, head_weight, teacher)
    div, grad_hidden, grad_head = pl.pallas_call(
        store,
        out_shape=(
            jax.ShapeDtypeStruct((1, 1), F32),
            jax.ShapeDtypeStruct((rows, width), BF16),
            jax.ShapeDtypeStruct((share, 4, piece), BF16),
        ),
        in_specs=[pl.BlockSpec(memory_space=vmem)] * 3,
        out_specs=(pl.BlockSpec(memory_space=vmem), anywhere, anywhere),
        scratch_shapes=[dma((STORES + 1,))],
        compiler_params=pltpu.CompilerParams(vmem_limit_bytes=1_000_000),
    )(*(pltpu.with_memory_space_constraint(x, vmem) for x in results))
    return div.reshape(()), grad_hidden, grad_head[:, None]


def solution(mesh):
    placed = (P("aa", None), P(None, "ba", None, None), P("ba", "aa", None, None))
    return jax.shard_map(
        functools.partial(on_device, mesh.shape["ba"]),
        mesh=mesh,
        in_specs=placed,
        out_specs=(P(), P("aa", None), P("aa", "ba", None, None)),
        check_vma=False,
    )
```

```python
import functools

import jax
import jax.numpy as jnp
from jax import lax
from jax.experimental import pallas as pl
from jax.experimental.pallas import tpu as pltpu
from jax.sharding import PartitionSpec as P

MESH = pl.DeviceIdType.MESH
F32 = jnp.float32
BF16 = jnp.bfloat16
grad_scale = 256.0
N_CHUNKS = 6
STORES = 6
HIDDEN_AT = 6
AHEAD = 3
LOADS_AFTER = 36
EARLY = 2
FIRST = 24
DIRECT = 2
TALK_AT = 1
ORDER = "c0,r0,h0,h1,h2,c1,r1,h3,s0,h4,h5"
ORDER_TAIL = "r2,p0,h6,s1,h7,m0,s2,q0,m1,c2,m2,c3,m3"
VMEM_LIMIT = 58_000_000
TB = 16
HALVES = 3


def finish(pending):
    for wait in pending:
        wait()


def ring(d, n):
    return min(d, n - d)


def offsets(y_size, x_size):
    steps = [(y, z, x) for y in range(y_size) for z in range(2) for x in range(x_size)]
    return sorted(steps, key=lambda s: -(ring(s[0], y_size) + 2 * s[1] + ring(s[2], x_size)))


def lanes_to_rows(row, n):
    return jnp.transpose(jnp.broadcast_to(row, (n, n)))


def kernel(
    n_ba, x_size,
    hid_hbm, w_hbm, t_hbm,
    div_ref, gh_out, gw_out,
    hid, w_raw, w_std, w_tr, t_raw, t_send, t_in, stu, lse_buf, n_send, n_in,
    hall, gall, acc, part, rs_buf, z_send, z_recv, fin, kl_p, kl_z, kl_a,
    in_sem, w_sem, t_ssem, t_rsem, n_ssem, n_rsem, h_ssem, h_rsem, s_ssem, s_rsem,
    g_ssem, g_rsem, r_ssem, r_rsem, z_ssem, z_rsem, a_ssem, a_rsem,
    kp_ssem, kp_rsem, kz_ssem, kz_rsem, ka_ssem, ka_rsem,
):
    a = lax.axis_index("aa")
    b = lax.axis_index("ba")
    width = hid.shape[1]
    rows = hid.shape[0]
    piece = w_raw.shape[3]
    per_a = n_ba // 4
    plane = n_ba // 2
    share = width // 4
    n_fb = plane // per_a
    fb_width = width // n_fb // HALVES
    chunk = w_raw.shape[1]
    t_owner = b // per_a
    t_slot = b % per_a
    y_size = n_ba // (2 * x_size)
    yy, zh, xx = b // (2 * x_size), (b // x_size) % 2, b % x_size
    p = yy * x_size + xx
    steps = offsets(y_size, x_size)
    plane_steps = [s for s in steps if s[1] == 0]

    def moved(step):
        y, z, x = step
        return (((yy + y) % y_size) * 2 + (zh + z) % 2) * x_size + (xx + x) % x_size

    half = a // 2

    def plane_peer(q):
        return ((q // x_size) * 2 + zh) * x_size + q % x_size

    b_across = plane_peer(p) + (1 - 2 * zh) * x_size
    core_mate = a + 1 - 2 * (a % 2)
    chip_mate = (a + 2) % 4

    def remote(src, dst, ssem, rsem, to_a, to_b):
        return pltpu.make_async_remote_copy(
            src_ref=src, dst_ref=dst, send_sem=ssem, recv_sem=rsem,
            device_id=(to_a, to_b), device_id_type=MESH,
        )

    pending = []

    def drain(sem, like):
        pending.append(remote(like, like, sem, sem, a, b).wait_send)

    def drain_t(sem, ref):
        def wait():
            @pl.when(t_owner == a)
            def _():
                remote(ref.at[: n_ba - 1], ref.at[: n_ba - 1], sem, sem, a, b).wait_send()

            @pl.when(t_owner != a)
            def _():
                remote(ref, ref, sem, sem, a, b).wait_send()

        pending.append(wait)

    t_load = pltpu.make_async_copy(t_hbm.at[:, 0], t_raw, in_sem.at[0])
    h_load = pltpu.make_async_copy(hid_hbm, hid, in_sem.at[1])
    t_load.start()

    def w_load(k):
        return pltpu.make_async_copy(
            w_hbm.at[pl.ds(k * chunk, chunk), 0], w_raw.at[k], w_sem.at[k]
        )

    barrier = pltpu.get_barrier_semaphore()

    def greet(to_a, to_b):
        pl.semaphore_signal(barrier, inc=1, device_id=(to_a, to_b), device_id_type=MESH)

    greetings = []
    for step in steps:
        hops = ring(step[0], y_size) + 2 * step[1] + ring(step[2], x_size)
        if hops:
            greetings.append((hops, 0, step))
    for da in range(4):
        for step in steps:
            if step[0] == 0:
                hops = ring(step[2], x_size) + (1 if da // 2 else 2 * step[1]) + 1
                greetings.append((hops, 1 + da, step))
    greetings.sort(key=lambda g: -g[0])

    def start_loads():
        h_load.start()
        for k in range(AHEAD):
            w_load(k).start()

    for n, (_, kind, step) in enumerate(greetings):
        if n == LOADS_AFTER:
            start_loads()
        if kind == 0:
            greet(a, moved(step))
            continue
        da = kind - 1
        src_a = ((half + da // 2) % 2) * 2 + (a + da) % 2
        src_b = (a * 2 + (zh + step[1]) % 2) * x_size + (xx + step[2]) % x_size
        if da or step != (0, 0, 0):
            greet(src_a, src_b)
        else:

            @pl.when(t_owner != a)
            def _():
                greet(src_a, src_b)

    b_near = moved((0, 1, 0))
    for step in range(1, 4):
        greet((a + step) % 4, b)
    for to_a in (chip_mate, 3 - a):
        greet(to_a, b_near)

    t_load.wait()
    t_send[...] = pltpu.einshape("tjr->jtr", t_raw[...])
    def t_max(j, m):
        return jnp.maximum(m, t_send[j].astype(F32))

    t_peak = lax.fori_loop(1, n_ba, t_max, t_send[0].astype(F32))
    t_peak = jnp.max(t_peak, axis=1, keepdims=True)

    def t_sum(j, s):
        return s + jnp.exp(t_send[j].astype(F32) - t_peak)

    t_total = lax.fori_loop(0, n_ba, t_sum, jnp.zeros((TB, piece), F32))
    t_lse = t_peak + jnp.log(jnp.sum(t_total, axis=1, keepdims=True))
    token = lax.broadcasted_iota(jnp.int32, (TB, rows), 0)
    lane = lax.broadcasted_iota(jnp.int32, (TB, rows), 1)
    n_send[...] = jnp.sum(
        jnp.where(lane == token + t_slot * TB, t_lse, 0.0), axis=0, keepdims=True
    )

    sub = chunk // 2

    def relayout(k, c):
        at = pl.ds(pl.multiple_of(k * sub, sub), sub)
        w_std[:, at, :] = pltpu.einshape(
            "dir->idr", w_raw[k // 2, pl.ds(pl.multiple_of((k % 2) * sub, sub), sub)]
        )
        return c

    t_dst = t_in.at[a, pl.ds(pl.multiple_of(t_slot * TB, TB), TB)]

    def to_owner(which, src_of, dst, ssem, rsem):
        for step in which:
            k = moved(step)
            copy = remote(src_of(k), dst, ssem, rsem, t_owner, k)
            if step != (0, 0, 0):
                copy.start()
            else:

                @pl.when(t_owner != a)
                def _():
                    copy.start()

                @pl.when(t_owner == a)
                def _():
                    pltpu.make_async_copy(src_of(k), dst, rsem).start()

    def talk():
        expected = 2 * n_ba - 1 + 5 - jnp.where(t_owner == a, 1, 0)
        pl.semaphore_wait(barrier, expected)
        to_owner(steps, lambda k: n_send, n_in.at[a, t_slot], n_ssem, n_rsem)
        to_owner(steps[:FIRST], lambda k: t_send.at[k], t_dst, t_ssem, t_rsem)

    drain_t(t_ssem, t_send)
    drain_t(n_ssem, lse_buf)
    early = jnp.logical_or(zh == 0, xx < EARLY)
    pl.when(jnp.logical_not(early))(talk)
    h_load.wait()
    for part_of in range(2):
        if part_of == TALK_AT:
            pl.when(early)(talk)
        for k in range(part_of * N_CHUNKS // 2, (part_of + 1) * N_CHUNKS // 2):
            w_load(k).wait()
            if k + AHEAD < N_CHUNKS:
                w_load(k + AHEAD).start()
            lax.fori_loop(2 * k, 2 * k + 2, relayout, 0)
        deep = slice(part_of * width // 2, (part_of + 1) * width // 2)
        for i in range(4):
            at = slice(i * piece, (i + 1) * piece)
            product = jnp.dot(hid[:, deep], w_std[i, deep], preferred_element_type=F32)
            stu[:, at] = product if part_of == 0 else stu[:, at] + product
    s = stu[...]
    s_peak = jnp.max(s, axis=1, keepdims=True)
    s_total = jnp.sum(jnp.exp(s - s_peak), axis=1, keepdims=True)
    s_part = s_peak + jnp.log(s_total)
    lse_buf[b] = jnp.transpose(jnp.broadcast_to(s_part, (rows, rows)))[0:1, :]

    for step in steps[:-1]:
        remote(lse_buf.at[b], lse_buf.at[b], s_ssem, s_rsem, a, moved(step)).start()
    drain(s_ssem, lse_buf.at[: n_ba - 1])
    to_owner(steps[FIRST:], lambda k: t_send.at[k], t_dst, t_ssem, t_rsem)

    mine = pl.ds(pl.multiple_of(a * rows, rows), rows)

    def h_part(to_a, to_b, start, size):
        src = hid_hbm.at[pl.ds(start, size), pl.ds(pl.multiple_of(to_a * share, share), share)]
        dst = hall.at[pl.ds(pl.multiple_of(a * rows + start, size), size)]
        return remote(src, dst, h_ssem, h_rsem, to_a, to_b)

    def send_hidden():
        for to_a in (chip_mate, 3 - a):
            h_part(to_a, b, 0, rows // 2).start()
            h_part(to_a, b_near, rows // 2, rows // 2).start()
        h_part(core_mate, b, 0, rows).start()
        own = hid_hbm.at[:, pl.ds(pl.multiple_of(a * share, share), share)]
        pltpu.make_async_copy(own, hall.at[mine], h_rsem).start()

    drain(h_ssem, hall.at[: 3 * rows])

    def turn(k, c):
        at = pl.ds(pl.multiple_of(k * sub, sub), sub)
        for i in range(4):
            w_tr[i, :, at] = jnp.transpose(w_std[i, at, :])
        return c

    lax.fori_loop(0, HIDDEN_AT, turn, 0)
    send_hidden()
    lax.fori_loop(HIDDEN_AT, 2 * N_CHUNKS, turn, 0)

    def arrived(sem, like):
        remote(like, like, sem, sem, a, b).wait_recv()

    arrived(t_rsem, t_in)
    arrived(n_rsem, n_in)
    arrived(s_rsem, lse_buf.at[: n_ba - 1])
    parts = lse_buf[...]
    s_top = jnp.max(parts, axis=0)
    s_lse = s_top + jnp.log(jnp.sum(jnp.exp(parts - s_top[None]), axis=0))
    s_lse = lanes_to_rows(s_lse, rows)[:, 0:1]

    t_parts = jnp.sum(n_in[...], axis=1)
    t_top = jnp.max(t_parts, axis=0)
    t_all = t_top + jnp.log(jnp.sum(jnp.exp(t_parts - t_top[None]), axis=0))
    t_all = lanes_to_rows(t_all, rows)[:, 0:1]

    def g_copy(i, src_a, to_a, ssem, rsem):
        at = pl.ds(pl.multiple_of(src_a * rows, rows), rows)
        return remote(gall.at[i, at], gall.at[i, at], ssem, rsem, to_a, b)

    def g_core(i):
        return g_copy(i, a, core_mate, g_ssem.at[0], g_rsem.at[0, i])

    def g_chip(i):
        return g_copy(i, a, chip_mate, g_ssem.at[1], g_rsem.at[1, i])

    def g_late(n):
        i, k = DIRECT + n // 4, n % 4
        at = pl.ds(pl.multiple_of(a * rows + k * (rows // 4), rows // 4), rows // 4)
        remote(gall.at[i, at], gall.at[i, at], g_ssem.at[1], g_rsem.at[1, i], chip_mate, b).start()

    def g_pass(i):
        return g_copy(i, chip_mate, core_mate, g_ssem.at[2], g_rsem.at[2, i])

    for k in range(3):
        drain(g_ssem.at[k], gall.at[:, mine])

    kl = jnp.zeros((rows, 128), F32)
    for i in range(4):
        log_target = t_in[i].astype(F32) - t_all
        log_student = stu[:, i * piece : (i + 1) * piece] - s_lse
        target_prob = jnp.exp(log_target)
        student_prob = jnp.exp(log_student)
        gall[i, mine, :] = (grad_scale * (student_prob - target_prob)).astype(BF16)
        term = target_prob * (log_target - log_student)
        for v in range(piece // 128):
            kl = kl + term[:, v * 128 : (v + 1) * 128]
        if i > 0:
            if i <= DIRECT:
                g_chip(i - 1).start()
            g_core(i - 1).start()
    kl_p[p] = jnp.sum(kl, axis=0, keepdims=True)
    g_core(3).start()

    def block_of(ref, q, f):
        return ref.at[
            pl.ds(pl.multiple_of((q % per_a) * TB, TB), TB),
            pl.ds(pl.multiple_of((f * n_fb + q // per_a) * fb_width, fb_width), fb_width),
        ]

    def to_plane(src_of, dst, ssem, rsem):
        for step in plane_steps[:-1]:
            q = ((yy + step[0]) % y_size) * x_size + (xx + step[2]) % x_size
            remote(src_of(q), dst, ssem, rsem, a, moved(step)).start()

    for f in range(HALVES):
        cols = slice(f * n_fb * fb_width, (f + 1) * n_fb * fb_width)
        total = None
        for i in range(4):
            term = jnp.dot(gall[i, mine, :], w_tr[i, :, cols], preferred_element_type=F32)
            total = term if total is None else total + term
        part[:, cols] = total.astype(BF16)
        to_plane(lambda q: block_of(part, q, f), rs_buf.at[f, p], r_ssem.at[f], r_rsem.at[f])
        pltpu.make_async_copy(block_of(part, p, f), rs_buf.at[f, p], r_rsem.at[f]).start()
        drain(r_ssem.at[f], rs_buf.at[f, : plane - 1])
    to_plane(lambda q: kl_p.at[p], kl_p.at[p], kp_ssem, kp_rsem)
    drain(kp_ssem, kl_p.at[: plane - 1])

    arrived(h_rsem, hall)
    near = pl.ds(pl.multiple_of(half * 2 * rows, 2 * rows), 2 * rows)
    far = pl.ds(pl.multiple_of((1 - half) * 2 * rows, 2 * rows), 2 * rows)

    def outer(i, at):
        return lax.dot_general(
            hall[at, :], gall[i, at, :], (((0,), (0,)), ((), ())), preferred_element_type=F32
        )

    def got_core(i):
        arrived(g_rsem.at[0, i], gall.at[i, mine])

    def got_chip(i):
        arrived(g_rsem.at[1, i], gall.at[i, mine])
        g_pass(i).start()

    def got_pass(i):
        arrived(g_rsem.at[2, i], gall.at[i, mine])

    for i in range(4):
        got_core(i)
        acc[i] = outer(i, near)
    def r_sums(f):
        arrived(r_rsem.at[f], rs_buf.at[f])

        def add(q, total):
            return total + rs_buf[f, q].astype(F32)

        total = lax.fori_loop(0, plane, add, jnp.zeros((TB, fb_width), F32))
        z_send[f] = total.astype(BF16)
        z_copy(f).start()
        drain(z_ssem.at[f], z_send.at[f])

    def z_copy(f):
        return remote(z_send.at[f], z_recv.at[f], z_ssem.at[f], z_rsem.at[f], a, b_across)

    def spread(f):
        z_copy(f).wait_recv()
        fin[f] = (z_send[f].astype(F32) + z_recv[f].astype(F32)).astype(BF16)
        to_plane(lambda q: fin.at[f], block_of(gh_out, p, f), a_ssem.at[f], a_rsem.at[f])
        pltpu.make_async_copy(fin.at[f], block_of(gh_out, p, f), a_rsem.at[f]).start()
        drain(a_ssem.at[f], rs_buf.at[f, : plane - 1])

    def kz_of(zz):
        return remote(kl_z.at[zz], kl_z.at[zz], kz_ssem, kz_rsem, a, b_across)

    def loss_plane(_):
        arrived(kp_rsem, kl_p.at[: plane - 1])
        kl_z[zh] = jnp.sum(kl_p[...], axis=0)
        kz_of(zh).start()

    def loss_across(_):
        kz_of(1 - zh).wait_recv()
        kl_a[a] = jnp.sum(kl_z[...], axis=0)
        for step in range(1, 4):
            remote(kl_a.at[a], kl_a.at[a], ka_ssem, ka_rsem, (a + step) % 4, b).start()

    drain(kz_ssem, kl_z.at[zh])
    drain(ka_ssem, kl_a.at[:3])

    def far_tokens(i):
        got_pass(i)
        w_std[i, 0:share, :] = (acc[i] + outer(i, far)).astype(BF16)

    for event in (ORDER + "," + ORDER_TAIL).split(","):
        {"c": got_chip, "r": r_sums, "s": spread, "h": g_late, "m": far_tokens,
            "p": loss_plane, "q": loss_across}[event[0]](
            int(event[1])
        )
    for k in range(share // sub):
        at = slice(k * sub, (k + 1) * sub)
        gw_out[at] = pltpu.einshape("idr->dir", w_std[:, at, :])
    arrived(ka_rsem, kl_a.at[:3])
    summed = jnp.sum(kl_a[...], axis=0)
    div_ref[...] = jnp.broadcast_to(
        jnp.sum(summed, axis=1, keepdims=True) / (4.0 * rows), div_ref.shape
    )
    half_width = width // HALVES
    for f in range(HALVES):
        arrived(a_rsem.at[f], gh_out.at[:, f * half_width : (f + 1) * half_width])
    finish(pending)


def store(div_in, gh_in, gw_in, div_ref, gh_hbm, gw_hbm, sem):
    n = gw_in.shape[0] // STORES
    copies = [
        pltpu.make_async_copy(
            gw_in.at[pl.ds(k * n, n)], gw_hbm.at[pl.ds(k * n, n)], sem.at[k]
        )
        for k in range(STORES)
    ]
    copies.append(pltpu.make_async_copy(gh_in, gh_hbm, sem.at[STORES]))
    for copy in copies:
        copy.start()
    div_ref[...] = div_in[0:1, 0:1]
    for copy in copies:
        copy.wait()


def on_device(n_ba, hidden, head_weight, teacher):
    rows, width = hidden.shape
    piece = head_weight.shape[3]
    share = width // 4
    plane = n_ba // 2
    per_a = n_ba // 4
    fb_width = width // (plane // per_a) // HALVES
    chunk = width // N_CHUNKS
    x_size = 4 if n_ba == 32 else 1
    dma = pltpu.SemaphoreType.DMA
    vmem, anywhere = pltpu.VMEM, pl.BlockSpec(memory_space=pl.ANY)
    results = pl.pallas_call(
        functools.partial(kernel, n_ba, x_size),
        out_shape=(
            vmem((8, 128), F32),
            vmem((rows, width), BF16),
            vmem((share, 4, piece), BF16),
        ),
        in_specs=[anywhere] * 3,
        out_specs=(pl.BlockSpec(memory_space=vmem),) * 3,
        scratch_shapes=[
            vmem((rows, width), BF16),
            vmem((N_CHUNKS, chunk, 4, piece), BF16),
            vmem((4, width, piece), BF16),
            vmem((4, piece, width), BF16),
            vmem((TB, n_ba, piece), BF16),
            vmem((n_ba, TB, piece), BF16),
            vmem((4, rows, piece), BF16),
            vmem((rows, 4 * piece), F32),
            vmem((n_ba, 1, rows), F32),
            vmem((1, rows), F32),
            vmem((4, per_a, 1, rows), F32),
            vmem((4 * rows, share), BF16),
            vmem((4, 4 * rows, piece), BF16),
            vmem((4, share, piece), F32),
            vmem((rows, width), BF16),
            vmem((HALVES, plane, TB, fb_width), BF16),
            vmem((HALVES, TB, fb_width), BF16),
            vmem((HALVES, TB, fb_width), BF16),
            vmem((HALVES, TB, fb_width), BF16),
            vmem((plane, 1, 128), F32),
            vmem((2, 1, 128), F32),
            vmem((4, 1, 128), F32),
            dma((2,)), dma((N_CHUNKS,)),
            dma, dma,
            dma, dma,
            dma, dma,
            dma, dma,
            dma((3,)), dma((3, 4)),
            dma((HALVES,)), dma((HALVES,)),
            dma((HALVES,)), dma((HALVES,)),
            dma((HALVES,)), dma((HALVES,)),
            dma, dma,
            dma, dma,
            dma, dma,
        ],
        compiler_params=pltpu.CompilerParams(
            collective_id=0, has_side_effects=True, vmem_limit_bytes=VMEM_LIMIT
        ),
    )(hidden, head_weight, teacher)
    div, grad_hidden, grad_head = pl.pallas_call(
        store,
        out_shape=(
            jax.ShapeDtypeStruct((1, 1), F32),
            jax.ShapeDtypeStruct((rows, width), BF16),
            jax.ShapeDtypeStruct((share, 4, piece), BF16),
        ),
        in_specs=[pl.BlockSpec(memory_space=vmem)] * 3,
        out_specs=(pl.BlockSpec(memory_space=vmem), anywhere, anywhere),
        scratch_shapes=[dma((STORES + 1,))],
        compiler_params=pltpu.CompilerParams(vmem_limit_bytes=1_000_000),
    )(*(pltpu.with_memory_space_constraint(x, vmem) for x in results))
    return div.reshape(()), grad_hidden, grad_head[:, None]


def solution(mesh):
    placed = (P("aa", None), P(None, "ba", None, None), P("ba", "aa", None, None))
    return jax.shard_map(
        functools.partial(on_device, mesh.shape["ba"]),
        mesh=mesh,
        in_specs=placed,
        out_specs=(P(), P("aa", None), P("aa", "ba", None, None)),
        check_vma=False,
    )
```
